32 devices in a mesh: gx: 2 (over x), gy: 4 (over z), gz: 4 (over y, core).
Axes of the slice: x: 2, y: 2, z: 4, core: 2. Of those that a mesh axis runs over, the one named last changes fastest.
Arguments:
- right_side: float32 [64, 256, 512], P('gx', 'gy', 'gz'), may hold values from -25 to 25
- coarse_inverse: float32 [256, 256], P(('gx', 'gy', 'gz')), may hold values from -0.07 to 0.07, as said below
- sphere_rows: bfloat16 [1536, 128], P(('gx', 'gy', 'gz')), may hold values from 0.5 to 8
- margin_block: int32 [1536, 1], P(('gx', 'gy', 'gz')), may hold values from 0 to 15; in each aligned block of 48 rows (0 to 47, 48 to 95, ...) at most 6 rows name the same one
- margin_column: int32 [1536], P(('gx', 'gy', 'gz')), may hold values from 0 to 2047
Outputs:
- pressure: float32 [64, 256, 512], P('gx', 'gy', 'gz')
- preconditioned: float32 [64, 256, 512], P('gx', 'gy', 'gz')
The draws below stay inside these ranges and needn't reach their ends.
Inputs may be any that keep to these rules, and one draw needn't show every extreme that they name: `margin_block`: in the rows of one device, no block is named by more than 6 rows, and some block is named by exactly 6. `coarse_inverse`: lower triangular with a positive diagonal.
All inputs are finite; a program needn't handle non-finite values.
Results may differ from the reference program's by a relative error of at most 0.0003.
Values may be sent and summed in bfloat16 or wider, within the bound.
No kernel may reach another device: no remote copies, remote signals or barrier semaphores. Data moves between devices by JAX's collectives and lax.ppermute only.
A program may use at most 64 MiB of HBM per device.

```python
import math
import jax
import jax.numpy as jnp
import numpy as np
from jax import lax

CX = 32
CY = 64
CZ = 128
SUB_DEV = 8
CHEB = 2
ITERS = 1
REC_DEV = 48
NX = 64
NY = 256
NZ = 512
NSUB = 256
CAP = 6
RECORDS = 1536
N_GX = 2
N_GY = 4
N_GZ = 4


def draw_right_side(key, part):
    key_base = jax.random.fold_in(key, 0)
    planes = jnp.arange(NX, dtype=jnp.float32)
    rising = (1.0 + 2.0 * planes / max(NX - 1, 1))[:, None, None]
    values = jnp.clip(jax.random.normal(key_base, (NX, NY, NZ), jnp.float32), -4.0, 4.0)
    return values * rising


def draw_coarse_inverse(key, part):
    key_off, key_diag = jax.random.split(key)
    row_place = jnp.arange(NSUB, dtype=jnp.int32)[:, None]
    col_place = jnp.arange(NSUB, dtype=jnp.int32)[None, :]
    offdiag = jnp.clip(jax.random.normal(key_off, (NSUB, NSUB), jnp.float32), -4.0, 4.0) * (0.03 / math.sqrt(NSUB))
    diagonal = 0.03 * jnp.exp(jax.random.uniform(key_diag, (NSUB,), jnp.float32, -0.7, 0.7))
    return jnp.where(col_place < row_place, offdiag, 0.0) + jnp.where(col_place == row_place, diagonal[:, None], 0.0)


def with_ends(drawn, key, least, largest):
    spot = [jax.random.randint(jax.random.fold_in(key, axis), (), 0, length) for axis, length in enumerate(drawn.shape)]
    main_axis = drawn.shape.index(max(drawn.shape))
    beside = spot[:main_axis] + [(spot[main_axis] + 1) % drawn.shape[main_axis]] + spot[main_axis + 1:]
    return drawn.at[tuple(spot)].set(least).at[tuple(beside)].set(largest)


def shard_levels(own_key, dims, pieces, least, top_value):
    factor_of = 1.0
    for axis_at, parts in pieces:
        steps = jax.random.uniform(jax.random.fold_in(jax.random.fold_in(own_key, 6), axis_at), (parts,), jnp.float32, least / len(pieces), top_value / len(pieces))
        factor_of = factor_of * jnp.repeat(jnp.exp(steps), dims[axis_at] // parts).reshape((-1,) + (1,) * (len(dims) - 1 - axis_at))
    return factor_of


def deal_out(own_key, own, number, rows, number_of, top, limit, skew):
    sequence = jax.random.permutation(own_key, number_of)
    crowded, usual = portions_of(number_of, rows * top, limit, skew, True), portions_of(number_of, rows * top, limit, skew, False)
    places = jnp.arange(number_of)

    def named(sizes, turn):
        used = int((sizes > 0).sum())
        fixed = max(1, used // 4)
        moved = fixed + (places - fixed + turn * (used - fixed)) % max(1, number_of - fixed)
        return jnp.zeros((number_of,), jnp.int32).at[sequence[jnp.where(places < fixed, places, moved)]].set(jnp.asarray(sizes, jnp.int32))

    sizes = jnp.where(number % 4 == 0, named(crowded, number // 4), named(usual, number - number // 4 - 1))
    mixed = jax.random.permutation(jax.random.fold_in(own, 3), number_of)
    giver, taker = mixed[0:number_of // 2 * 2:2], mixed[1:number_of // 2 * 2:2]
    slack = jnp.minimum(sizes[giver] - 1, limit - sizes[taker]) // 2
    slack = jnp.where((giver == sequence[0]) | (taker == sequence[0]) | (sizes[taker] == 0), 0, jnp.maximum(slack, 0))
    moved = jax.random.randint(jax.random.fold_in(own, 4), (number_of // 2,), 0, 1 << 20) % (slack + 1)
    sizes = sizes.at[giver].add(-moved).at[taker].add(moved)
    items = jnp.searchsorted(jnp.cumsum(sizes), jnp.arange(rows * top), side="right").astype(jnp.int32)
    listing = items.reshape(top, rows).T
    listing = listing[jax.random.permutation(jax.random.fold_in(own, 1), rows)]
    turn = jax.random.randint(jax.random.fold_in(own, 2), (rows, 1), 0, top)
    return jnp.take_along_axis(listing, (jnp.arange(top)[None, :] + turn) % top, axis=1)


def portions_of(amount, total, limit, slope, full):
    portions = [(1 << 20) // math.isqrt(standing ** slope) + 1 for standing in range(1, amount + 1)]
    largest = limit if full else min(limit, max(-(-total // amount), total * portions[0] // sum(portions)))
    least = 1 if total - largest >= amount - 1 else 0
    given, spare = [largest] + [least] * (amount - 1), total - largest - least * (amount - 1)
    while spare > 0:
        free = [i for i in range(1, amount) if given[i] < largest] or [i for i in range(1, amount) if given[i] < limit]
        mass, remaining = sum([portions[i] for i in free]), spare
        for i in free:
            addition = min(limit - given[i], max(1, remaining * portions[i] // mass), spare)
            given[i] = given[i] + addition
            spare = spare - addition
    return np.array(given)


def setup_inputs(seed: int = 0) -> dict:
    keys = jax.random.split(jax.random.key(seed), 6)
    right_side = draw_right_side(jax.random.fold_in(keys[5], 71), 0)
    coarse_inverse = draw_coarse_inverse(jax.random.fold_in(keys[5], 71), 0)
    sphere_rows = jnp.clip(jnp.exp(math.log(8.0) - 2.7725887 * jax.random.uniform(keys[2], (RECORDS, CZ), jnp.float32) ** shard_levels(keys[2], (RECORDS, CZ), ((0, 32),), -0.2, 0.2)), 0.5, 8.0).astype(jnp.bfloat16)
    margin_block_keys = jax.random.split(jax.random.fold_in(keys[3], 1), RECORDS // REC_DEV)
    margin_block_turns = jax.random.permutation(jax.random.fold_in(keys[3], 3), RECORDS // REC_DEV)
    margin_block = jax.vmap(lambda own, number: deal_out(jax.random.fold_in(keys[3], 2), own, number, REC_DEV, N_GY * N_GZ, 1, CAP, 2))(margin_block_keys, margin_block_turns).reshape((RECORDS, 1))
    margin_column = with_ends(jax.random.randint(keys[4], (RECORDS,), 0, CX * CY), jax.random.fold_in(keys[4], 1), 0, (CX * CY) - 1).astype(jnp.int32)
    return dict(right_side=right_side, coarse_inverse=coarse_inverse, sphere_rows=sphere_rows, margin_block=margin_block, margin_column=margin_column)


bound_low = 0.1
bound_high = 2.0


def face_terms(density):
    padded = jnp.pad(density, 1)
    return (2.0 / (density + padded[:-2, 1:-1, 1:-1]), 2.0 / (density + padded[2:, 1:-1, 1:-1]),
            2.0 / (density + padded[1:-1, :-2, 1:-1]), 2.0 / (density + padded[1:-1, 2:, 1:-1]),
            2.0 / (density + padded[1:-1, 1:-1, :-2]), 2.0 / (density + padded[1:-1, 1:-1, 2:]))


def apply_operator(field, faces, diagonal):
    padded = jnp.pad(field, 1)
    beside = faces[0] * padded[:-2, 1:-1, 1:-1] + faces[1] * padded[2:, 1:-1, 1:-1]
    beside = beside + faces[2] * padded[1:-1, :-2, 1:-1] + faces[3] * padded[1:-1, 2:, 1:-1]
    beside = beside + faces[4] * padded[1:-1, 1:-1, :-2] + faces[5] * padded[1:-1, 1:-1, 2:]
    return diagonal * field - beside


def chebyshev(residual, faces, diagonal):
    centre_value = 0.5 * (bound_high + bound_low)
    spread = 0.5 * (bound_high - bound_low)
    sigma_ratio = centre_value / spread
    weight_old = 1.0 / sigma_ratio
    update = residual / diagonal / centre_value
    result = update
    for sweep in range(CHEB - 1):
        weight_new = 1.0 / (2.0 * sigma_ratio - weight_old)
        update = (weight_new * weight_old) * update + (2.0 * weight_new / spread) * ((residual - apply_operator(result, faces, diagonal)) / diagonal)
        result = result + update
        weight_old = weight_new
    return result


def coarse_part(residual, coarse_inverse):
    shaped = residual.reshape(N_GX, CX, N_GY, CY, N_GZ, SUB_DEV, CZ // SUB_DEV)
    sums = jnp.sum(shaped, axis=(1, 3, 6)).reshape(-1)
    inner = jnp.dot(coarse_inverse, sums, precision=lax.Precision.HIGHEST)
    coarse_values = jnp.dot(inner, coarse_inverse, precision=lax.Precision.HIGHEST)
    spread_out = jnp.broadcast_to(coarse_values.reshape(N_GX, 1, N_GY, 1, N_GZ, SUB_DEV, 1),
                                  (N_GX, CX, N_GY, CY, N_GZ, SUB_DEV, CZ // SUB_DEV))
    return spread_out.reshape(NX, NY, NZ)


def reference(right_side, coarse_inverse, sphere_rows, margin_block, margin_column):
    record_count = sphere_rows.shape[0]
    source_x = jnp.arange(record_count, dtype=jnp.int32) // (REC_DEV * N_GY * N_GZ)
    target = margin_block[:, 0]
    block_y = target // N_GZ
    block_z = target % N_GZ
    cell_x = margin_column // CY
    cell_y = margin_column % CY
    grid = jnp.zeros((N_GX, CX, N_GY, CY, N_GZ, CZ), jnp.float32)
    grid = grid.at[source_x, cell_x, block_y, cell_y, block_z].add(sphere_rows.astype(jnp.float32))
    density = 1.0 + grid.reshape(NX, NY, NZ)
    faces = face_terms(density)
    diagonal = faces[0] + faces[1] + faces[2] + faces[3] + faces[4] + faces[5]

    def precondition(residual):
        return chebyshev(residual, faces, diagonal) + coarse_part(residual, coarse_inverse)

    pressure = jnp.zeros_like(right_side)
    residual = right_side
    preconditioned = precondition(residual)
    direction = preconditioned
    gamma = jnp.sum(residual * preconditioned)
    for step in range(ITERS):
        image = apply_operator(direction, faces, diagonal)
        alpha = gamma / jnp.sum(direction * image)
        pressure = pressure + alpha * direction
        residual = residual - alpha * image
        preconditioned = precondition(residual)
        if step + 1 < ITERS:
            gamma_new = jnp.sum(residual * preconditioned)
            direction = preconditioned + (gamma_new / gamma) * direction
            gamma = gamma_new
    return pressure, preconditioned
```

```python
import jax
import jax.numpy as jnp
from jax import lax
from jax.sharding import PartitionSpec as P

bound_low = 0.1
bound_high = 2.0


def with_halo(value, sides, width):
    for axis, dim in sides:
        size, length = (lax.axis_size(axis), value.shape[dim])
        up = [(i, (i + 1) % size) for i in range(size - 1)]
        down = [(j, i) for i, j in up]
        last = lax.slice_in_dim(value, length - width, length, axis=dim)
        initial = lax.slice_in_dim(value, 0, width, axis=dim)
        before = lax.ppermute(last, axis, up)
        after = lax.ppermute(initial, axis, down)
        value = jnp.concatenate([before, value, after], axis=dim)
    return value


def face_terms(density, padded):
    return (
        2.0 / (density + padded[:-2, 1:-1, 1:-1]),
        2.0 / (density + padded[2:, 1:-1, 1:-1]),
        2.0 / (density + padded[1:-1, :-2, 1:-1]),
        2.0 / (density + padded[1:-1, 2:, 1:-1]),
        2.0 / (density + padded[1:-1, 1:-1, :-2]),
        2.0 / (density + padded[1:-1, 1:-1, 2:]),
    )


def apply_operator(field, faces, diagonal):
    padded = with_halo(field, (("gx", 0), ("gy", 1), ("gz", 2)), 1)
    beside = faces[0] * padded[:-2, 1:-1, 1:-1] + faces[1] * padded[2:, 1:-1, 1:-1]
    beside = beside + faces[2] * padded[1:-1, :-2, 1:-1] + faces[3] * padded[1:-1, 2:, 1:-1]
    beside = beside + faces[4] * padded[1:-1, 1:-1, :-2] + faces[5] * padded[1:-1, 1:-1, 2:]
    return diagonal * field - beside


def chebyshev(residual, faces, diagonal):
    centre_value = 0.5 * (bound_high + bound_low)
    spread = 0.5 * (bound_high - bound_low)
    sigma_ratio = centre_value / spread
    weight_old = 1.0 / sigma_ratio
    update = residual / diagonal / centre_value
    result = update
    weight_new = 1.0 / (2.0 * sigma_ratio - weight_old)
    update = weight_new * weight_old * update + 2.0 * weight_new / spread * (
        (residual - apply_operator(result, faces, diagonal)) / diagonal
    )
    result = result + update
    return result


def doubling_steps():
    steps = []
    for axis in ("gy", "gx", "gz"):
        size = lax.axis_size(axis)
        stride = 1
        while stride < size:
            steps.append((axis, stride))
            stride *= 2
    return steps


def gather_all(value):
    sizes = {axis: lax.axis_size(axis) for axis in ("gx", "gy", "gz")}
    value = value[None]
    for axis in ("gy", "gx", "gz"):
        size, stride = (sizes[axis], 1)
        index = lax.axis_index(axis)
        value = value[None]
        while stride < size:
            other = lax.ppermute(value, axis, [(i, i ^ stride) for i in range(size)])
            upper = (index // stride) % 2
            value = jnp.where(
                upper == 1,
                jnp.concatenate([other, value], axis=0),
                jnp.concatenate([value, other], axis=0),
            )
            stride *= 2
        value = value.reshape((-1,) + value.shape[2:]) if axis == "gy" else value
    value = value.reshape((sizes["gz"], sizes["gx"], sizes["gy"]) + value.shape[3:])
    value = jnp.moveaxis(value, 0, 2)
    return value.reshape((-1,) + value.shape[3:])


def sum_all(value):
    for axis, stride in doubling_steps():
        size = lax.axis_size(axis)
        value = value + lax.ppermute(value, axis, [(i, i ^ stride) for i in range(size)])
    return value


def coarse_part(residual, whole_inverse, slabs):
    size_x, size_y, size_z = residual.shape
    local_sums = jnp.sum(residual.reshape(size_x, size_y, slabs, size_z // slabs), axis=(0, 1, 3))
    sums = gather_all(jnp.broadcast_to(local_sums[:, None], (slabs, 128)))[:, :, 0].reshape(-1)
    inner = jnp.dot(whole_inverse, sums, precision=lax.Precision.HIGHEST)
    place = (lax.axis_index("gx") * lax.axis_size("gy") + lax.axis_index("gy")) * lax.axis_size("gz") + lax.axis_index("gz")
    own = lax.dynamic_slice_in_dim(whole_inverse, place * slabs, slabs, axis=1)
    coarse_values = jnp.dot(inner, own, precision=lax.Precision.HIGHEST)
    spread_out = jnp.broadcast_to(
        coarse_values.reshape(1, 1, slabs, 1), (size_x, size_y, slabs, size_z // slabs)
    )
    return spread_out.reshape(size_x, size_y, size_z)


def gather_density(sphere_rows, margin_block, margin_column, columns, size_z):
    groups_y = lax.axis_size("gy")
    groups_z = lax.axis_size("gz")
    targets = groups_y * groups_z
    records = sphere_rows.shape[0]
    capacity = max(2, 2 * records // targets)
    target = margin_block[:, 0]
    onehot = (target[:, None] == jnp.arange(targets, dtype=jnp.int32)[None, :]).astype(jnp.int32)
    earlier = jnp.cumsum(onehot, axis=0) - onehot
    slot_index = jnp.sum(earlier * onehot, axis=1)
    position = target * capacity + slot_index
    send_rows = jnp.zeros((targets * capacity, size_z), jnp.bfloat16).at[position].set(sphere_rows)
    send_columns = jnp.zeros((targets * capacity,), jnp.int32).at[position].set(margin_column)
    got_rows, got_columns = (
        lax.all_to_all(
            send_rows.reshape(targets, capacity, size_z),
            ("gy", "gz"),
            split_axis=0,
            concat_axis=0,
            tiled=True,
        ),
        lax.all_to_all(
            send_columns.reshape(targets, capacity),
            ("gy", "gz"),
            split_axis=0,
            concat_axis=0,
            tiled=True,
        ),
    )
    added = (
        jnp.zeros((columns, size_z), jnp.float32)
        .at[got_columns.reshape(-1)]
        .add(got_rows.reshape(-1, size_z).astype(jnp.float32))
    )
    return 1.0 + added


def shards(right_side, coarse_inverse, sphere_rows, margin_block, margin_column):
    size_x, size_y, size_z = right_side.shape
    density = gather_density(
        sphere_rows, margin_block, margin_column, size_x * size_y, size_z
    ).reshape(size_x, size_y, size_z)
    padded = with_halo(density, (("gx", 0), ("gy", 1), ("gz", 2)), 1)
    faces = face_terms(density, padded)
    diagonal = faces[0] + faces[1] + faces[2] + faces[3] + faces[4] + faces[5]

    slabs = coarse_inverse.shape[0]
    whole_inverse = gather_all(coarse_inverse).reshape(-1, coarse_inverse.shape[1])

    def precondition(residual):
        return chebyshev(residual, faces, diagonal) + coarse_part(residual, whole_inverse, slabs)

    residual = right_side
    preconditioned = precondition(residual)
    direction = preconditioned
    image = apply_operator(direction, faces, diagonal)
    both = jnp.stack([jnp.sum(residual * preconditioned), jnp.sum(direction * image)])
    both = sum_all(jnp.broadcast_to(both[:, None], (2, 128)))
    alpha = both[0, 0] / both[1, 0]
    pressure = alpha * direction
    residual = residual - alpha * image
    preconditioned = precondition(residual)
    return (pressure, preconditioned)


def solution(mesh):
    placed = (
        P("gx", "gy", "gz"),
        P(("gx", "gy", "gz"), None),
        P(("gx", "gy", "gz"), None),
        P(("gx", "gy", "gz"), None),
        P(("gx", "gy", "gz")),
    )
    return jax.shard_map(
        shards,
        mesh=mesh,
        in_specs=placed,
        out_specs=(P("gx", "gy", "gz"), P("gx", "gy", "gz")),
        check_vma=False,
    )
```

```python
import functools

import jax
import jax.numpy as jnp
from jax import lax
from jax.experimental import pallas as pl
from jax.experimental.pallas import tpu as pltpu
from jax.sharding import PartitionSpec as P

bound_low = 0.1
bound_high = 2.0
theta = 0.5 * (bound_high + bound_low)
delta = 0.5 * (bound_high - bound_low)
weight_first = delta / theta
weight_second = 1.0 / (2.0 * theta / delta - weight_first)
far = 2.0 * weight_second / delta
near = 1.0 + weight_second * weight_first + far * (theta - 1.0)

AXES = ("gx", "gy", "gz")
LANES = 128
REACH = 4
SUBS = 8
SLOT = 64
EXACT = lax.Precision.HIGHEST
VMEM = pl.BlockSpec(memory_space=pltpu.VMEM)


def lane_of(rows):
    return lax.broadcasted_iota(jnp.int32, (rows, LANES), 1)


def row_of(rows):
    return lax.broadcasted_iota(jnp.int32, (rows, LANES), 0)


def message_rows(records, halves):
    meta = 16 * pl.cdiv(3 + 3 * halves, 16)
    return records, records + 8 * halves, records + 16 * halves, meta


def place_sums(total, device, slabs):
    width = LANES // slabs
    base = lax.rem(device, width) * slabs
    source = lax.broadcasted_iota(jnp.int32, (LANES, LANES), 0)
    target = lax.broadcasted_iota(jnp.int32, (LANES, LANES), 1)
    first = (target - base) * width
    chosen = (source >= first) & (source < first + width) & (target >= base) & (target < base + slabs)
    return jnp.dot(total, chosen.astype(jnp.float32), precision=EXACT, preferred_element_type=jnp.float32)


def device_number(sizes):
    return (lax.axis_index("gx") * sizes[1] + lax.axis_index("gy")) * sizes[2] + lax.axis_index("gz")


def pack_kernel(sizes, residual_ref, inverse_ref, rows_ref, block_ref, column_ref, out_ref, index_ref):
    size_x, size_y, _ = residual_ref.shape
    slabs, subdomains = inverse_ref.shape
    records = rows_ref.shape[0]
    halves = subdomains // LANES
    high_at, low_at, meta_at, meta_rows = message_rows(records, halves)
    out_ref[0:records, :] = rows_ref[...]
    whole = jnp.concatenate([inverse_ref[:, h * LANES : (h + 1) * LANES] for h in range(halves)], axis=0)
    high = whole.astype(jnp.bfloat16)
    out_ref[high_at : high_at + 8 * halves, :] = high
    out_ref[low_at : low_at + 8 * halves, :] = (whole - high.astype(jnp.float32)).astype(jnp.bfloat16)

    index_ref[...] = jnp.zeros_like(index_ref)
    index_ref[0:1, 0:records] = block_ref[...].astype(jnp.float32) + 1.0
    column = column_ref[...].astype(jnp.float32)
    plane = jnp.floor((column + 0.5) * (1.0 / size_y))
    index_ref[1:2, 0:records] = plane + (lax.axis_index("gx") * size_x).astype(jnp.float32)
    index_ref[2:3, 0:records] = column - plane * size_y

    total = lax.fori_loop(
        1, size_x, lambda i, acc: acc + residual_ref[i], residual_ref[0], unroll=4
    )
    total = jnp.broadcast_to(jnp.sum(total, axis=0, keepdims=True), (8, LANES))
    device = device_number(sizes)
    sums = place_sums(total, device, slabs)[0:1]
    high = sums.astype(jnp.bfloat16).astype(jnp.float32)
    middle = (sums - high).astype(jnp.bfloat16).astype(jnp.float32)
    low = sums - high - middle
    half = device // (LANES // slabs)
    row = row_of(meta_rows)
    meta = jnp.where(row == 0, index_ref[0:1, :], 0.0)
    meta = jnp.where(row == 1, index_ref[1:2, :], meta)
    meta = jnp.where(row == 2, index_ref[2:3, :], meta)
    meta = jnp.where(row == 3 + half, high, meta)
    meta = jnp.where(row == 3 + halves + half, middle, meta)
    meta = jnp.where(row == 3 + 2 * halves + half, low, meta)
    out_ref[meta_at : meta_at + meta_rows, :] = meta.astype(jnp.bfloat16)


def margin_y_kernel(residual_ref, above_ref, below_ref, down_ref, up_ref):
    size_x, size_y, _ = residual_ref.shape
    row = row_of(8)

    def plane(x, at):
        tile = pl.ds(at, 8)
        if x < size_x:
            return residual_ref[x, tile, :]
        x -= size_x
        return above_ref[x, tile, :] if x < REACH else below_ref[x - REACH, tile, :]

    for pair in range((size_x + 2 * REACH) // 2):
        one, two = 2 * pair, 2 * pair + 1
        down_ref[pair] = jnp.where(row < 4, plane(one, 0), pltpu.roll(plane(two, 0), 4, 0))
        up_ref[pair] = jnp.where(row < 4, pltpu.roll(plane(two, size_y - 8), 4, 0), plane(one, size_y - 8))


def margin_z_kernel(residual_ref, above_ref, below_ref, after_ref, before_ref, wide_ref, edge_ref):
    size_x, size_y, _ = residual_ref.shape
    wide_y = size_y + 2 * REACH
    row = row_of(8)
    place = lane_of(wide_y) % 16
    sub_of = lane_of(wide_y) // 16
    for x in range(size_x + 2 * REACH):
        if x < size_x:
            wide_ref[x, 0:size_y, :] = residual_ref[x]
        elif x < size_x + REACH:
            wide_ref[x, 0:size_y, :] = above_ref[x - size_x]
        else:
            wide_ref[x, 0:size_y, :] = below_ref[x - size_x - REACH]
        after, before = after_ref[x // 2], before_ref[x // 2]
        if x % 2:
            after, before = pltpu.roll(after, 4, 0), pltpu.roll(before, 4, 0)
        wide_ref[x, size_y:wide_y, :] = jnp.where(row < 4, after, before)

    def group(g, carry):
        edge = jnp.zeros((wide_y, LANES), jnp.float32)
        for sub in range(SUBS):
            value = wide_ref[g * SUBS + sub]
            first = pltpu.roll(value, (sub * 16 + 4) % LANES, 1)
            last = pltpu.roll(value, (sub * 16 + 8 + 4) % LANES, 1)
            edge = jnp.where((sub_of == sub) & (place >= 4) & (place < 8), first, edge)
            edge = jnp.where((sub_of == sub) & (place >= 8) & (place < 12), last, edge)
        edge_ref[g] = edge
        return carry

    lax.fori_loop(0, edge_ref.shape[0], group, 0)


def coarse_solve(message_refs, high_at, low_at, halves, sums):
    def body(message_ref, i, total):
        high = message_ref[i, high_at : high_at + 8 * halves, :].astype(jnp.float32)
        low = message_ref[i, low_at : low_at + 8 * halves, :].astype(jnp.float32)
        rows = high + low
        tiles = [rows[8 * h : 8 * h + 8] for h in range(halves)]
        inner = sum(tiles[h] * sums[h] for h in range(halves))
        inner = jnp.sum(inner, axis=1, keepdims=True)
        return tuple(total[h] + inner * tiles[h] for h in range(halves))

    zero = jnp.zeros((8, LANES), jnp.float32)
    total = (zero,) * halves
    for ref in message_refs:
        total = lax.fori_loop(0, ref.shape[0], functools.partial(body, ref), total, unroll=8)
    return [jnp.broadcast_to(jnp.sum(t, axis=0, keepdims=True), (8, LANES)) for t in total]


def pick(values, device, slab, slabs):
    per_half = LANES // slabs
    half = device // per_half
    chosen = values[0]
    for h in range(1, len(values)):
        chosen = jnp.where(half == h, values[h], chosen)
    index = lax.rem(device, per_half) * slabs + slab
    return jnp.take_along_axis(chosen, index, axis=1)


def main_kernel(
    sizes, records, halves, slabs, size_x, size_y,
    message_ref, other_ref, wide_ref, edge_ref, lower_ref, upper_ref,
    direction_ref, applied_ref, stat_ref,
    key_ref, code_ref, turned_ref, left_ref, right_ref, added_ref,
    density_ref, x_ref, y_ref, z_ref, h_ref, u_ref, d_ref, inside_ref, coarse_ref,
):
    n_gx, n_gy, n_gz = sizes
    gx, gy, gz = (lax.axis_index(a) for a in AXES)
    half = message_ref.shape[0]
    wide_x, wide_y = size_x + 2 * REACH, size_y + 2 * REACH
    groups = wide_x // SUBS
    high_at, low_at, meta_at, meta_rows = message_rows(records, halves)
    f32, bf16 = jnp.float32, jnp.bfloat16
    lane = lane_of(wide_y)
    row = row_of(wide_y)
    place = lane % 16
    sub_of = lane // 16

    def roll(value, shift, axis):
        return pltpu.roll(value, shift, axis)

    def read_meta(i, total):
        for j, ref in enumerate((message_ref, other_ref)):
            tile = ref[i, meta_at : meta_at + meta_rows, :].astype(f32)
            for k in range(3):
                key_ref[k, pl.ds(i + j * half, 1), :] = tile[k : k + 1]
            total = total + tile
        return total

    total = lax.fori_loop(0, half, read_meta, jnp.zeros((meta_rows, LANES), f32), unroll=4)
    sums = [
        total[3 + h : 4 + h] + total[3 + halves + h : 4 + halves + h] + total[3 + 2 * halves + h : 4 + 2 * halves + h]
        for h in range(halves)
    ]
    coarse = coarse_solve((message_ref, other_ref), high_at, low_at, halves, sums)

    def there(ix, iy, iz):
        ok = (ix >= 0) & (ix < n_gx) & (iy >= 0) & (iy < n_gy) & (iz >= 0) & (iz < n_gz)
        return ok.astype(f32), jnp.where(ok, (ix * n_gy + iy) * n_gz + iz, 0)

    lane8 = lane_of(8)
    row8 = row_of(8)
    place8 = lane8 % 16
    constant = lambda k: jnp.full((8, LANES), k, jnp.int32)

    def main_values(ix, iy):
        ok, device = there(ix, iy, gz)
        return jnp.full((8, LANES), ok, f32), ok * pick(coarse, device, lane8 // (LANES // slabs), slabs)

    def edge_values(ix, iy):
        parts = []
        for iz, slab in ((gz - 1, slabs - 1), (gz, 0), (gz, slabs - 1), (gz + 1, 0)):
            ok, device = there(ix, iy, iz)
            parts.append((jnp.full((8, LANES), ok, f32), ok * pick(coarse, device, constant(slab), slabs)))
        out = []
        for k in range(2):
            value = jnp.where(place8 < 4, parts[0][k], parts[1][k])
            value = jnp.where(place8 >= 8, parts[2][k], value)
            out.append(jnp.where(place8 >= 12, parts[3][k], value))
        return out

    def fill(kind, values_at):
        own, after, before = values_at(gy), values_at(gy + 1), values_at(gy - 1)
        for k, ref in enumerate((inside_ref, coarse_ref)):
            ref[kind, 0:size_y, :] = jnp.concatenate([own[k]] * (size_y // 8), axis=0)
            ref[kind, size_y:wide_y, :] = jnp.where(row8 < 4, after[k], before[k])

    def beside_x(iy):
        above, below = edge_values(gx + 1, iy), edge_values(gx - 1, iy)
        return [jnp.where(lane8 < 4 * 16, a, b) for a, b in zip(above, below)]

    fill(0, lambda iy: main_values(gx, iy))
    fill(1, lambda iy: main_values(gx + 1, iy))
    fill(2, lambda iy: main_values(gx - 1, iy))
    fill(3, lambda iy: edge_values(gx, iy))
    fill(4, beside_x)

    block, plane, line = (key_ref[k, 0:half, :] + roll(key_ref[k, half : 2 * half, :], SLOT, 1) for k in range(3))
    valid = block > 0.5
    block = block - 1.0
    block_y = jnp.floor((block + 0.5) * (1.0 / n_gz))
    side = block - block_y * n_gz - gz.astype(f32)
    at_x = plane - (gx * size_x).astype(f32)
    at_y = (block_y - gy.astype(f32)) * size_y + line
    valid = valid & (at_x >= -REACH) & (at_x < size_x + REACH) & (at_y >= -REACH) & (at_y < size_y + REACH)
    at_x = jnp.where(at_x < 0, at_x + wide_x, at_x)
    at_y = jnp.where(at_y < 0, at_y + wide_y, at_y)
    at_group = jnp.floor((at_x + 0.5) * (1.0 / SUBS))
    at_sub = at_x - at_group * SUBS
    code_ref[...] = jnp.where(valid, at_group * wide_y + at_y, -1.0)
    turned_ref[...] = jnp.full(turned_ref.shape, -1.0, f32)
    turned_ref[0, 0:half, :] = jnp.where(side == 0, at_sub, -1.0)
    turned_ref[1, 0:half, :] = jnp.where((side >= -1) & (side <= 1), at_sub + SUBS * (side + 1), -1.0)
    turned_ref[0] = turned_ref[0].T
    turned_ref[1] = turned_ref[1].T

    chunk = min(half, 16)
    rows_all = left_ref.shape[0]
    row_number = lax.broadcasted_iota(jnp.int32, (rows_all, LANES), 0).astype(f32)
    source = lax.broadcasted_iota(jnp.int32, (LANES, LANES), 0)
    target = lax.broadcasted_iota(jnp.int32, (LANES, LANES), 1)
    wanted = jnp.where(target % 8 < 4, target % 4 + (LANES - 4), target % 4)
    chooser = (source == wanted).astype(bf16)
    kind = jnp.where(target % 16 < 4, 0, jnp.where(target % 16 < 12, 1, 2))
    edge_code = (target // 16 + SUBS * kind).astype(f32)

    for c in range(half // chunk):
        def build(q, carry, c=c):
            p = q + c * chunk
            at = pl.ds(pl.multiple_of(q * LANES, LANES), LANES)
            code = code_ref[pl.ds(p, 1), :]
            left_ref[:, at] = jnp.where(row_number == code, 1.0, 0.0).astype(bf16)
            rows = jnp.concatenate([message_ref[p, 0:SLOT, :], other_ref[p, 0:SLOT, :]], axis=0)
            turn = lax.rem(LANES - p, LANES)
            key = jnp.broadcast_to(roll(turned_ref[0], turn, 1)[:, 0:1], (LANES, LANES))
            edge_key = jnp.broadcast_to(roll(turned_ref[1], turn, 1)[:, 0:1], (LANES, LANES))
            wide_rows = rows.astype(f32)
            for sub in range(SUBS):
                right_ref[at, sub * LANES : (sub + 1) * LANES] = jnp.where(key == sub, wide_rows, 0.0).astype(bf16)
            edges = jnp.dot(rows, chooser, preferred_element_type=f32)
            right_ref[at, SUBS * LANES :] = jnp.where(edge_key == edge_code, edges, 0.0).astype(bf16)
            return carry

        lax.fori_loop(0, chunk, build, 0)
        for n in range(0, SUBS + 1, 2):
            columns = slice(n * LANES, min(n + 2, SUBS + 1) * LANES)
            product = jnp.dot(left_ref[...], right_ref[:, columns], preferred_element_type=f32)
            added_ref[:, columns] = product if c == 0 else added_ref[:, columns] + product

    def kind_of(x):
        return jnp.where(x < size_x, 0, jnp.where(x < size_x + REACH, 1, 2))

    for g in range(groups):
        lines = slice(g * wide_y, (g + 1) * wide_y)
        for sub in range(SUBS):
            x = g * SUBS + sub
            k = 0 if x < size_x else 1 if x < size_x + REACH else 2
            density_ref[x] = inside_ref[k] + added_ref[lines, sub * LANES : (sub + 1) * LANES]
        k = 3 if g < groups - 1 else 4
        density_ref[wide_x + g] = inside_ref[k] + added_ref[lines, SUBS * LANES :]

    def z_after(value, edges, sub):
        return jnp.where(lane == LANES - 1, roll(edges, 115 - 16 * sub, 1), roll(value, LANES - 1, 1))

    def z_before(value, edges, sub):
        return jnp.where(lane == 0, roll(edges, 125 - 16 * sub, 1), roll(value, 1, 1))

    def y_after(value):
        return roll(value, wide_y - 1, 0)

    def y_before(value):
        return roll(value, 1, 0)

    def edge_x_after(ref, g):
        other = ref[wide_x + (g + 1) % groups]
        return jnp.where(lane >= LANES - 16, roll(other, LANES - 16, 1), roll(ref[wide_x + g], LANES - 16, 1))

    def edge_x_before(ref, g):
        other = ref[wide_x + (g - 1) % groups]
        return jnp.where(lane < 16, roll(other, 16, 1), roll(ref[wide_x + g], 16, 1))

    def following(x):
        return jnp.where(x + 1 == wide_x, 0, x + 1)

    def preceding(x):
        return jnp.where(x == 0, wide_x - 1, x - 1)

    def beta(one, two):
        return 2.0 / jnp.maximum(one + two, 0.5)

    for g in range(groups):
        j = wide_x + g
        value = density_ref[j]
        x_ref[j] = beta(value, edge_x_after(density_ref, g))
        y_ref[j] = beta(value, y_after(value))
        z_ref[j] = beta(value, roll(value, LANES - 1, 1))

    for g in range(groups):
        j = wide_x + g
        k = 3 if g < groups - 1 else 4
        diagonal = x_ref[j] + edge_x_before(x_ref, g) + y_ref[j] + y_before(y_ref[j]) + z_ref[j] + roll(z_ref[j], 1, 1)
        h_ref[j] = inside_ref[k] / diagonal
        residual = edge_ref[g]
        residual = jnp.where(place < 4, roll(lower_ref[g], LANES - 8, 1), residual)
        residual = jnp.where(place >= 12, roll(upper_ref[g], 8, 1), residual)
        u_ref[j] = residual * h_ref[j] * (1.0 / theta)

    def faces(x, carry):
        value = density_ref[x]
        x_ref[x] = beta(value, density_ref[following(x)])
        y_ref[x] = beta(value, y_after(value))
        z_ref[x] = beta(value, z_after(value, density_ref[wide_x + x // SUBS], lax.rem(x, SUBS)))
        return carry

    lax.fori_loop(0, wide_x, faces, 0)

    def scale(x, carry):
        along_y, along_z = y_ref[x], z_ref[x]
        diagonal = x_ref[x] + x_ref[preceding(x)] + along_y + y_before(along_y)
        diagonal = diagonal + along_z + z_before(along_z, z_ref[wide_x + x // SUBS], lax.rem(x, SUBS))
        h = inside_ref[kind_of(x)] / diagonal
        h_ref[x] = h
        u_ref[x] = wide_ref[x] * h * (1.0 / theta)
        return carry

    lax.fori_loop(0, wide_x, scale, 0)

    def smooth(ref, x):
        value, along_y, along_z = ref[x], y_ref[x], z_ref[x]
        j, sub = wide_x + x // SUBS, lax.rem(x, SUBS)
        before = preceding(x)
        beside = x_ref[x] * ref[following(x)] + x_ref[before] * ref[before]
        beside = beside + along_y * y_after(value) + y_before(along_y * value)
        beside = beside + along_z * z_after(value, ref[j], sub) + z_before(along_z * value, z_ref[j] * ref[j], sub)
        return near * value + far * (h_ref[x] * beside)

    def edge_smooth(ref, g):
        j = wide_x + g
        value = ref[j]
        product = x_ref[j] * value
        before = x_ref[wide_x + (g - 1) % groups] * ref[wide_x + (g - 1) % groups]
        beside = x_ref[j] * edge_x_after(ref, g) + jnp.where(lane < 16, roll(before, 16, 1), roll(product, 16, 1))
        beside = beside + y_ref[j] * y_after(value) + y_before(y_ref[j] * value)
        beside = beside + z_ref[j] * roll(value, LANES - 1, 1) + roll(z_ref[j] * value, 1, 1)
        return near * value + far * (h_ref[j] * beside)

    for g in range(groups):
        d_ref[wide_x + g] = edge_smooth(u_ref, g) + coarse_ref[3 if g < groups - 1 else 4]

    def direct(x, carry):
        d_ref[x] = smooth(u_ref, x) + coarse_ref[kind_of(x)]
        return carry

    lax.fori_loop(0, wide_x, direct, 0)

    for g in range(groups):
        j = wide_x + g
        value = d_ref[j]
        flux_y = y_ref[j] * (value - y_after(value))
        flux_z = z_ref[j] * (value - roll(value, LANES - 1, 1))
        image = x_ref[j] * (value - edge_x_after(d_ref, g))
        image = image + edge_x_before(x_ref, g) * (value - edge_x_before(d_ref, g))
        image = image + (flux_y - y_before(flux_y)) + (flux_z - roll(flux_z, 1, 1))
        u_ref[j] = image * h_ref[j] * (1.0 / theta)

    def image_of(x):
        value = d_ref[x]
        j, sub = wide_x + x // SUBS, lax.rem(x, SUBS)
        before = preceding(x)
        edges = d_ref[j]
        edge_flux = z_ref[j] * (edges - roll(edges, LANES - 1, 1))
        flux_y = y_ref[x] * (value - y_after(value))
        flux_z = z_ref[x] * (value - z_after(value, edges, sub))
        image = x_ref[x] * (value - d_ref[following(x)]) + x_ref[before] * (value - d_ref[before])
        image = image + (flux_y - y_before(flux_y)) + (flux_z - z_before(flux_z, edge_flux, sub))
        u_ref[x] = image * h_ref[x] * (1.0 / theta)
        return value, image

    def image_own(x, carry):
        value, image = image_of(x)
        value, image = value[0:size_y], image[0:size_y]
        direction_ref[x] = value
        return (
            carry[0] + wide_ref[x, 0:size_y, :] * value,
            carry[1] + value * image,
            carry[2] + image,
        )

    zero = jnp.zeros((size_y, LANES), f32)
    found = lax.fori_loop(0, size_x, image_own, (zero, zero, zero))
    image_of(size_x)
    image_of(wide_x - 1)

    device = device_number(sizes)
    folded = [jnp.sum(f, axis=0, keepdims=True) for f in found]
    image_sums = place_sums(jnp.broadcast_to(folded[2], (8, LANES)), device, slabs)[0:1]
    gamma = jnp.sum(folded[0], axis=1, keepdims=True)
    curvature = jnp.sum(folded[1], axis=1, keepdims=True)
    last = jnp.where(lane8[0:1] == 0, gamma, jnp.where(lane8[0:1] == 1, curvature, 0.0))
    own_half = device // (LANES // slabs)

    def spread(i, carry):
        for h in range(halves):
            stat_ref[i, h : h + 1, :] = jnp.where(own_half == h, image_sums, 0.0)
        stat_ref[i, halves : halves + 1, :] = last
        return carry

    lax.fori_loop(0, stat_ref.shape[0], spread, 0, unroll=4)

    def second(x, carry):
        applied_ref[x] = smooth(u_ref, x)[0:size_y]
        return carry

    lax.fori_loop(0, size_x, second, 0)


def finish_kernel(
    sizes, records, halves, slabs,
    stat_ref, message_ref, other_ref, direction_ref, applied_ref, pressure_ref, preconditioned_ref,
):
    high_at, low_at, _, _ = message_rows(records, halves)
    total = lax.fori_loop(
        1, stat_ref.shape[0], lambda i, acc: acc + stat_ref[i], stat_ref[0], unroll=4
    )
    sums = [total[h : h + 1] for h in range(halves)]
    coarse = coarse_solve((message_ref, other_ref), high_at, low_at, halves, sums)
    lane8 = lane_of(8)
    own = pick(coarse, device_number(sizes), lane8 // (LANES // slabs), slabs)
    last = total[halves : halves + 1]
    alpha = last[:, 0:1] / last[:, 1:2]
    size_x, size_y, _ = direction_ref.shape
    alpha = jnp.broadcast_to(alpha, (size_y, LANES))
    own = jnp.concatenate([own] * (size_y // 8), axis=0)

    def body(x, carry):
        direction = direction_ref[x]
        pressure_ref[x] = alpha * direction
        preconditioned_ref[x] = direction - alpha * (applied_ref[x] + own)
        return carry

    lax.fori_loop(0, size_x, body, 0, unroll=2)


def cycle(value, axis, step):
    size = lax.axis_size(axis)
    return lax.ppermute(value, axis, [(i, (i + step) % size) for i in range(size)])


def exchange(value, axis, stride):
    size = lax.axis_size(axis)
    return lax.ppermute(value, axis, [(i, i ^ stride) for i in range(size)])


def doublings():
    steps = []
    for axis in ("gy", "gx", "gz"):
        strides = [1 << k for k in range(lax.axis_size(axis).bit_length() - 1)]
        steps += [(axis, stride) for stride in (strides[::-1] if axis == "gz" else strides)]
    return steps


def shards(sizes, right_side, coarse_inverse, sphere_rows, margin_block, margin_column):
    size_x, size_y, size_z = right_side.shape
    slabs, subdomains = coarse_inverse.shape
    records = sphere_rows.shape[0]
    halves = subdomains // LANES
    devices = sizes[0] * sizes[1] * sizes[2]
    wide_x, wide_y = size_x + 2 * REACH, size_y + 2 * REACH
    groups = wide_x // SUBS
    planes = wide_x + groups
    f32, bf16 = jnp.float32, jnp.bfloat16
    _, _, meta_at, meta_rows = message_rows(records, halves)
    shape = jax.ShapeDtypeStruct

    def call(kernel, out_shape, operands, scratch=()):
        many = isinstance(out_shape, tuple)
        return pl.pallas_call(
            kernel,
            out_shape=out_shape,
            in_specs=[VMEM] * len(operands),
            out_specs=tuple(VMEM for _ in out_shape) if many else VMEM,
            scratch_shapes=list(scratch),
        )(*operands)

    message = call(
        functools.partial(pack_kernel, sizes),
        shape((meta_at + meta_rows, LANES), bf16),
        (right_side, coarse_inverse, sphere_rows, margin_block.reshape(1, records), margin_column.reshape(1, records)),
        (pltpu.VMEM((8, LANES), f32),),
    )
    steps = doublings()
    held = message[None]
    received = exchange(held, *steps[0])
    first, last = right_side[:REACH], right_side[size_x - REACH :]
    if sizes[0] == 2:
        above = below = cycle(jnp.where(lax.axis_index("gx") == 0, last, first), "gx", 1)
    else:
        above, below = cycle(first, "gx", -1), cycle(last, "gx", 1)
    held, received, above, below = lax.optimization_barrier((held, received, above, below))
    held = jnp.concatenate([held, received], axis=0)
    received = exchange(held, *steps[1])
    pairs = shape((wide_x // 2, 8, LANES), f32)
    down, up = call(margin_y_kernel, (pairs, pairs), (right_side, above, below))
    after, before = cycle(down, "gy", -1), cycle(up, "gy", 1)
    held, received, after, before = lax.optimization_barrier((held, received, after, before))
    held = jnp.concatenate([held, received], axis=0)
    received = exchange(held, *steps[2])
    wide, edge = call(
        margin_z_kernel,
        (shape((wide_x, wide_y, LANES), f32), shape((groups, wide_y, LANES), f32)),
        (right_side, above, below, after, before),
    )
    held, received, edge = lax.optimization_barrier((held, received, edge))
    lower, upper = cycle(edge, "gz", 1), cycle(edge, "gz", -1)
    for step in steps[3:]:
        held = jnp.concatenate([held, received], axis=0)
        received = exchange(held, *step)

    half = devices // 2
    depth = min(half, 16) * LANES
    rows_all = 16 * pl.cdiv(groups * wide_y, 16)
    field = pltpu.VMEM((planes, wide_y, LANES), f32)
    kinds = pltpu.VMEM((5, wide_y, LANES), f32)
    block = shape((size_x, size_y, LANES), f32)
    direction, applied, stats = call(
        functools.partial(main_kernel, sizes, records, halves, slabs, size_x, size_y),
        (block, block, shape((devices, halves + 1, LANES), f32)),
        (held, received, wide, edge, lower, upper),
        (
            pltpu.VMEM((3, devices, LANES), f32),
            pltpu.VMEM((half, LANES), f32),
            pltpu.VMEM((2, LANES, LANES), f32),
            pltpu.VMEM((rows_all, depth), bf16),
            pltpu.VMEM((depth, (SUBS + 1) * LANES), bf16),
            pltpu.VMEM((rows_all, (SUBS + 1) * LANES), f32),
            field, field, field, field, field, field, field, kinds, kinds,
        ),
    )
    stats = lax.all_to_all(stats, AXES, 0, 0, tiled=True)
    return call(
        functools.partial(finish_kernel, sizes, records, halves, slabs),
        (block, block),
        (stats, held, received, direction, applied),
    )


def solution(mesh):
    placed = (
        P("gx", "gy", "gz"),
        P(("gx", "gy", "gz"), None),
        P(("gx", "gy", "gz"), None),
        P(("gx", "gy", "gz"), None),
        P(("gx", "gy", "gz")),
    )
    sizes = tuple(mesh.shape[axis] for axis in AXES)
    return jax.shard_map(
        functools.partial(shards, sizes),
        mesh=mesh,
        in_specs=placed,
        out_specs=(P("gx", "gy", "gz"), P("gx", "gy", "gz")),
        check_vma=False,
    )
```

```python
import functools

import jax
import jax.numpy as jnp
from jax import lax
from jax.experimental import pallas as pl
from jax.experimental.pallas import tpu as pltpu
from jax.sharding import PartitionSpec as P


bound_low = 0.1
bound_high = 2.0
theta = 0.5 * (bound_high + bound_low)
delta = 0.5 * (bound_high - bound_low)
weight_first = delta / theta
weight_second = 1.0 / (2.0 * theta / delta - weight_first)
far = 2.0 * weight_second / delta
near = 1.0 + weight_second * weight_first + far * (theta - 1.0)

AXES = ("gx", "gy", "gz")
LANES = 128
REACH = 4
SUBS = 8
SLOT = 64
EXACT = lax.Precision.HIGHEST
VMEM = pl.BlockSpec(memory_space=pltpu.VMEM)


def lane_of(rows):
    return lax.broadcasted_iota(jnp.int32, (rows, LANES), 1)


def row_of(rows):
    return lax.broadcasted_iota(jnp.int32, (rows, LANES), 0)


def message_rows(records, halves):
    meta = 16 * pl.cdiv(3 + 3 * halves, 16)
    return records, records + 8 * halves, records + 16 * halves, meta


def place_sums(total, device, slabs):
    width = LANES // slabs
    base = lax.rem(device, width) * slabs
    source = lax.broadcasted_iota(jnp.int32, (LANES, LANES), 0)
    target = lax.broadcasted_iota(jnp.int32, (LANES, LANES), 1)
    first = (target - base) * width
    chosen = (source >= first) & (source < first + width) & (target >= base) & (target < base + slabs)
    return jnp.dot(total, chosen.astype(jnp.float32), precision=EXACT, preferred_element_type=jnp.float32)


def device_number(sizes):
    return (lax.axis_index("gx") * sizes[1] + lax.axis_index("gy")) * sizes[2] + lax.axis_index("gz")


def pack_kernel(sizes, residual_ref, inverse_ref, rows_ref, block_ref, column_ref, out_ref, index_ref):
    size_x, size_y, _ = residual_ref.shape
    slabs, subdomains = inverse_ref.shape
    records = rows_ref.shape[0]
    halves = subdomains // LANES
    high_at, low_at, meta_at, meta_rows = message_rows(records, halves)
    out_ref[0:records, :] = rows_ref[...]
    whole = jnp.concatenate([inverse_ref[:, h * LANES : (h + 1) * LANES] for h in range(halves)], axis=0)
    high = whole.astype(jnp.bfloat16)
    out_ref[high_at : high_at + 8 * halves, :] = high
    out_ref[low_at : low_at + 8 * halves, :] = (whole - high.astype(jnp.float32)).astype(jnp.bfloat16)

    index_ref[...] = jnp.zeros_like(index_ref)
    index_ref[0:1, 0:records] = block_ref[...].astype(jnp.float32) + 1.0
    column = column_ref[...].astype(jnp.float32)
    plane = jnp.floor((column + 0.5) * (1.0 / size_y))
    index_ref[1:2, 0:records] = plane + (lax.axis_index("gx") * size_x).astype(jnp.float32)
    index_ref[2:3, 0:records] = column - plane * size_y

    total = lax.fori_loop(
        1, size_x, lambda i, acc: acc + residual_ref[i], residual_ref[0], unroll=4
    )
    total = jnp.broadcast_to(jnp.sum(total, axis=0, keepdims=True), (8, LANES))
    device = device_number(sizes)
    sums = place_sums(total, device, slabs)[0:1]
    high = sums.astype(jnp.bfloat16).astype(jnp.float32)
    middle = (sums - high).astype(jnp.bfloat16).astype(jnp.float32)
    low = sums - high - middle
    half = device // (LANES // slabs)
    row = row_of(meta_rows)
    meta = jnp.where(row == 0, index_ref[0:1, :], 0.0)
    meta = jnp.where(row == 1, index_ref[1:2, :], meta)
    meta = jnp.where(row == 2, index_ref[2:3, :], meta)
    meta = jnp.where(row == 3 + half, high, meta)
    meta = jnp.where(row == 3 + halves + half, middle, meta)
    meta = jnp.where(row == 3 + 2 * halves + half, low, meta)
    out_ref[meta_at : meta_at + meta_rows, :] = meta.astype(jnp.bfloat16)


def margin_y_kernel(residual_ref, above_ref, below_ref, down_ref, up_ref):
    size_x, size_y, _ = residual_ref.shape
    row = row_of(8)

    def plane(x, at):
        if x < size_x:
            return residual_ref[x, pl.ds(at, 8), :]
        x -= size_x
        return above_ref[x, pl.ds(at, 8), :] if x < REACH else below_ref[x - REACH, pl.ds(at, 8), :]

    for pair in range((size_x + 2 * REACH) // 2):
        low = [plane(2 * pair + k, 0) for k in range(2)]
        high = [plane(2 * pair + k, size_y - 8) for k in range(2)]
        down_ref[pair] = jnp.where(row < 4, low[0], pltpu.roll(low[1], 4, 0))
        up_ref[pair] = jnp.where(row < 4, pltpu.roll(high[1], 4, 0), high[0])


def edge_group(values):
    rows = values[0].shape[0]
    place, sub_of = lane_of(rows) % 16, lane_of(rows) // 16
    edge = jnp.zeros((rows, LANES), jnp.float32)
    for sub, value in enumerate(values):
        first = pltpu.roll(value, (sub * 16 + 4) % LANES, 1)
        last = pltpu.roll(value, (sub * 16 + 12) % LANES, 1)
        edge = jnp.where((sub_of == sub) & (place >= 4) & (place < 8), first, edge)
        edge = jnp.where((sub_of == sub) & (place >= 8) & (place < 12), last, edge)
    return edge


def edge_own_kernel(residual_ref, above_ref, below_ref, edge_ref):
    groups = edge_ref.shape[0]

    def group(g, carry):
        edge_ref[g] = edge_group([residual_ref[g * SUBS + sub] for sub in range(SUBS)])
        return carry

    lax.fori_loop(0, groups - 1, group, 0)
    edge_ref[groups - 1] = edge_group([ref[i] for ref in (above_ref, below_ref) for i in range(REACH)])


def edge_tail_kernel(part_ref, after_ref, before_ref, tail_ref, edge_ref):
    groups, size_y, _ = part_ref.shape
    row = row_of(8)
    for g in range(groups):
        tails = []
        for x in range(g * SUBS, g * SUBS + SUBS):
            after, before = after_ref[x // 2], before_ref[x // 2]
            if x % 2:
                after, before = pltpu.roll(after, 4, 0), pltpu.roll(before, 4, 0)
            tails.append(jnp.where(row < 4, after, before))
            tail_ref[x] = tails[-1]
        edge_ref[g, 0:size_y, :] = part_ref[g]
        edge_ref[g, size_y:, :] = edge_group(tails)


def coarse_solve(message_refs, high_at, low_at, halves, sums):
    def body(message_ref, i, total):
        high = message_ref[i, high_at : high_at + 8 * halves, :].astype(jnp.float32)
        low = message_ref[i, low_at : low_at + 8 * halves, :].astype(jnp.float32)
        rows = high + low
        tiles = [rows[8 * h : 8 * h + 8] for h in range(halves)]
        inner = sum(tiles[h] * sums[h] for h in range(halves))
        inner = jnp.sum(inner, axis=1, keepdims=True)
        return tuple(total[h] + inner * tiles[h] for h in range(halves))

    zero = jnp.zeros((8, LANES), jnp.float32)
    total = (zero,) * halves
    for ref in message_refs:
        total = lax.fori_loop(0, ref.shape[0], functools.partial(body, ref), total, unroll=8)
    return [jnp.broadcast_to(jnp.sum(t, axis=0, keepdims=True), (8, LANES)) for t in total]


def pick(values, device, slab, slabs):
    per_half = LANES // slabs
    half = device // per_half
    chosen = values[0]
    for h in range(1, len(values)):
        chosen = jnp.where(half == h, values[h], chosen)
    index = lax.rem(device, per_half) * slabs + slab
    return jnp.take_along_axis(chosen, index, axis=1)


def main_kernel(
    sizes, records, halves, slabs, size_x, size_y,
    message_ref, other_ref, residual_ref, above_ref, below_ref, tail_ref, edge_ref, lower_ref, upper_ref,
    direction_ref, applied_ref, stat_ref,
    key_ref, code_ref, turned_ref, left_ref, right_ref, added_ref,
    density_ref, x_ref, y_ref, z_ref, h_ref, u_ref, d_ref, inside_ref, coarse_ref, first_ref, second_ref, third_ref, fourth_ref,
):
    n_gx, n_gy, n_gz = sizes
    gx, gy, gz = (lax.axis_index(a) for a in AXES)
    half = message_ref.shape[0]
    wide_x, wide_y = size_x + 2 * REACH, size_y + 2 * REACH
    groups = wide_x // SUBS
    high_at, low_at, meta_at, meta_rows = message_rows(records, halves)
    f32, bf16 = jnp.float32, jnp.bfloat16
    lane = lane_of(wide_y)
    row = row_of(wide_y)
    place = lane % 16

    def roll(value, shift, axis):
        return pltpu.roll(value, shift, axis)

    def read_meta(i, total):
        for j, ref in enumerate((message_ref, other_ref)):
            tile = ref[i, meta_at : meta_at + meta_rows, :].astype(f32)
            for k in range(3):
                key_ref[k, pl.ds(i + j * half, 1), :] = tile[k : k + 1]
            total = total + tile
        return total

    total = lax.fori_loop(0, half, read_meta, jnp.zeros((meta_rows, LANES), f32), unroll=4)
    sums = [
        total[3 + h : 4 + h] + total[3 + halves + h : 4 + halves + h] + total[3 + 2 * halves + h : 4 + 2 * halves + h]
        for h in range(halves)
    ]
    coarse = coarse_solve((message_ref, other_ref), high_at, low_at, halves, sums)

    def there(ix, iy, iz):
        ok = (ix >= 0) & (ix < n_gx) & (iy >= 0) & (iy < n_gy) & (iz >= 0) & (iz < n_gz)
        return ok.astype(f32), jnp.where(ok, (ix * n_gy + iy) * n_gz + iz, 0)

    lane8 = lane_of(8)
    row8 = row_of(8)
    place8 = lane8 % 16
    constant = lambda k: jnp.full((8, LANES), k, jnp.int32)

    def main_values(ix, iy):
        ok, device = there(ix, iy, gz)
        return jnp.full((8, LANES), ok, f32), ok * pick(coarse, device, lane8 // (LANES // slabs), slabs)

    def edge_values(ix, iy):
        parts = []
        for iz, slab in ((gz - 1, slabs - 1), (gz, 0), (gz, slabs - 1), (gz + 1, 0)):
            ok, device = there(ix, iy, iz)
            parts.append((jnp.full((8, LANES), ok, f32), ok * pick(coarse, device, constant(slab), slabs)))
        out = []
        for k in range(2):
            value = jnp.where(place8 < 4, parts[0][k], parts[1][k])
            value = jnp.where(place8 >= 8, parts[2][k], value)
            out.append(jnp.where(place8 >= 12, parts[3][k], value))
        return out

    def fill(kind, values_at):
        own, after, before = values_at(gy), values_at(gy + 1), values_at(gy - 1)
        for k, ref in enumerate((inside_ref, coarse_ref)):
            ref[kind, 0:size_y, :] = jnp.concatenate([own[k]] * (size_y // 8), axis=0)
            ref[kind, size_y:wide_y, :] = jnp.where(row8 < 4, after[k], before[k])

    def beside_x(iy):
        above, below = edge_values(gx + 1, iy), edge_values(gx - 1, iy)
        return [jnp.where(lane8 < 4 * 16, a, b) for a, b in zip(above, below)]

    fill(0, lambda iy: main_values(gx, iy))
    fill(1, lambda iy: main_values(gx + 1, iy))
    fill(2, lambda iy: main_values(gx - 1, iy))
    fill(3, lambda iy: edge_values(gx, iy))
    fill(4, beside_x)

    block, plane, line = (key_ref[k, 0:half, :] + roll(key_ref[k, half : 2 * half, :], SLOT, 1) for k in range(3))
    valid = block > 0.5
    block = block - 1.0
    block_y = jnp.floor((block + 0.5) * (1.0 / n_gz))
    side = block - block_y * n_gz - gz.astype(f32)
    at_x = plane - (gx * size_x).astype(f32)
    at_y = (block_y - gy.astype(f32)) * size_y + line
    valid = valid & (at_x >= -REACH) & (at_x < size_x + REACH) & (at_y >= -REACH) & (at_y < size_y + REACH)
    at_x = jnp.where(at_x < 0, at_x + wide_x, at_x)
    at_y = jnp.where(at_y < 0, at_y + wide_y, at_y)
    at_group = jnp.floor((at_x + 0.5) * (1.0 / SUBS))
    at_sub = at_x - at_group * SUBS
    code_ref[...] = jnp.where(valid, at_group * wide_y + at_y, -1.0)
    turned_ref[...] = jnp.full(turned_ref.shape, -1.0, f32)
    turned_ref[0, 0:half, :] = jnp.where(side == 0, at_sub, -1.0)
    turned_ref[1, 0:half, :] = jnp.where((side >= -1) & (side <= 1), at_sub + SUBS * (side + 1), -1.0)
    turned_ref[0] = turned_ref[0].T
    turned_ref[1] = turned_ref[1].T

    chunk = min(half, 16)
    rows_all = left_ref.shape[0]
    row_number = lax.broadcasted_iota(jnp.int32, (rows_all, LANES), 0).astype(f32)
    source = lax.broadcasted_iota(jnp.int32, (LANES, LANES), 0)
    target = lax.broadcasted_iota(jnp.int32, (LANES, LANES), 1)
    wanted = jnp.where(target % 8 < 4, target % 4 + (LANES - 4), target % 4)
    chooser = (source == wanted).astype(bf16)
    kind = jnp.where(target % 16 < 4, 0, jnp.where(target % 16 < 12, 1, 2))
    edge_code = (target // 16 + SUBS * kind).astype(f32)

    for c in range(half // chunk):
        def build(q, carry, c=c):
            p = q + c * chunk
            at = pl.ds(pl.multiple_of(q * LANES, LANES), LANES)
            code = code_ref[pl.ds(p, 1), :]
            left_ref[:, at] = jnp.where(row_number == code, 1.0, 0.0).astype(bf16)
            rows = jnp.concatenate([message_ref[p, 0:SLOT, :], other_ref[p, 0:SLOT, :]], axis=0)
            turn = lax.rem(LANES - p, LANES)
            key = jnp.broadcast_to(roll(turned_ref[0], turn, 1)[:, 0:1], (LANES, LANES))
            edge_key = jnp.broadcast_to(roll(turned_ref[1], turn, 1)[:, 0:1], (LANES, LANES))
            wide_rows = rows.astype(f32)
            for sub in range(SUBS):
                right_ref[at, sub * LANES : (sub + 1) * LANES] = jnp.where(key == sub, wide_rows, 0.0).astype(bf16)
            edges = jnp.dot(rows, chooser, preferred_element_type=f32)
            right_ref[at, SUBS * LANES :] = jnp.where(edge_key == edge_code, edges, 0.0).astype(bf16)
            return carry

        lax.fori_loop(0, chunk, build, 0)
        for n in range(0, SUBS + 1, 2):
            columns = slice(n * LANES, min(n + 2, SUBS + 1) * LANES)
            product = jnp.dot(left_ref[...], right_ref[:, columns], preferred_element_type=f32)
            added_ref[:, columns] = product if c == 0 else added_ref[:, columns] + product

    for g in range(groups):
        lines = slice(g * wide_y, (g + 1) * wide_y)
        for sub in range(SUBS):
            x = g * SUBS + sub
            k = 0 if x < size_x else 1 if x < size_x + REACH else 2
            density_ref[x] = inside_ref[k] + added_ref[lines, sub * LANES : (sub + 1) * LANES]
        k = 3 if g < groups - 1 else 4
        density_ref[wide_x + g] = inside_ref[k] + added_ref[lines, SUBS * LANES :]

    def y_after(value):
        return roll(value, wide_y - 1, 0)

    def y_before(value):
        return roll(value, 1, 0)

    def joined(after, before):
        return jnp.where(place == 13, roll(before, 10, 1), after)

    def z_after(value, edges):
        return jnp.where(lane == LANES - 1, edges, roll(value, LANES - 1, 1))

    def z_before(value, edges):
        return jnp.where(lane == 0, edges, roll(value, 1, 1))

    def edge_x_after(value, other):
        return jnp.where(lane >= LANES - 16, roll(other, LANES - 16, 1), roll(value, LANES - 16, 1))

    def edge_x_before(value, other):
        return jnp.where(lane < 16, roll(other, 16, 1), roll(value, 16, 1))

    def sweep(reach, body, carry, joined_ref, beside=None):
        def turned(g, sub):
            return roll(joined_ref[g], 115 - 16 * sub, 1)

        for x in range(-reach, 0):
            after = wide_x + x + 1 if x < -1 else 0
            carry = body(wide_x + x, after, 2, turned(groups - 1, SUBS + x), carry)

        def group(g, carry):
            if beside:
                beside(g, jnp.where(g == 0, groups - 1, g - 1), g + 1, 3)
            for sub in range(SUBS):
                x = g * SUBS + sub
                carry = body(x, x + 1, 0, turned(g, sub), carry)
            return carry

        carry = lax.fori_loop(0, groups - 1, group, carry)
        if beside:
            beside(groups - 1, groups - 2, 0, 4)
        for x in range(reach):
            carry = body(size_x + x, size_x + x + 1, 1, turned(groups - 1, x), carry)
        return carry

    def beta(one, two):
        return 2.0 / jnp.maximum(one + two, 0.5)

    for g in range(groups):
        j = wide_x + g
        value = density_ref[j]
        x_ref[j] = beta(value, edge_x_after(value, density_ref[wide_x + (g + 1) % groups]))
        y_ref[j] = beta(value, y_after(value))
        z_ref[j] = beta(value, roll(value, LANES - 1, 1))

    for g in range(groups):
        j = wide_x + g
        before_x = edge_x_before(x_ref[j], x_ref[wide_x + (g - 1) % groups])
        diagonal = x_ref[j] + before_x + y_ref[j] + y_before(y_ref[j]) + z_ref[j] + roll(z_ref[j], 1, 1)
        h = inside_ref[3 if g < groups - 1 else 4] / diagonal
        h_ref[j] = h
        residual = edge_ref[g]
        residual = jnp.where(place < 4, roll(lower_ref[g], LANES - 8, 1), residual)
        residual = jnp.where(place >= 12, roll(upper_ref[g], 8, 1), residual)
        u_ref[j] = residual * h * (1.0 / theta)
        first_ref[g] = joined(density_ref[j], z_ref[j])

    def edge_direct(g, before_g, after_g, k):
        j, before_j, after_j = wide_x + g, wide_x + before_g, wide_x + after_g
        value, along_x, along_y, along_z = u_ref[j], x_ref[j], y_ref[j], z_ref[j]
        product_z = along_z * value
        beside = along_x * edge_x_after(value, u_ref[after_j])
        beside = beside + edge_x_before(along_x * value, x_ref[before_j] * u_ref[before_j])
        beside = beside + along_y * y_after(value) + y_before(along_y * value)
        beside = beside + along_z * roll(value, LANES - 1, 1) + roll(product_z, 1, 1)
        d_ref[j] = near * value + far * (h_ref[j] * beside) + coarse_ref[k]
        second_ref[g] = joined(value, product_z)

    def edge_image(g, before_g, after_g, k):
        j, before_j, after_j = wide_x + g, wide_x + before_g, wide_x + after_g
        value, before = d_ref[j], d_ref[before_j]
        flux_x = x_ref[j] * (value - edge_x_after(value, d_ref[after_j]))
        flux_y = y_ref[j] * (value - y_after(value))
        flux_z = z_ref[j] * (value - roll(value, LANES - 1, 1))
        image = flux_x + edge_x_before(x_ref[j], x_ref[before_j]) * (value - edge_x_before(value, before))
        image = image + (flux_y - y_before(flux_y)) + (flux_z - roll(flux_z, 1, 1))
        image = image * h_ref[j] * (1.0 / theta)
        third_ref[g] = joined(value, flux_z)
        fourth_ref[g] = joined(image, z_ref[j] * image)

    def faces(x, after, k, edges, before):
        value = density_ref[x]
        along_x = beta(value, density_ref[after])
        along_y = beta(value, y_after(value))
        along_z = beta(value, z_after(value, edges))
        diagonal = before + along_x + along_y + y_before(along_y) + along_z + z_before(along_z, edges)
        h = inside_ref[k] / diagonal
        x_ref[x], y_ref[x], z_ref[x], h_ref[x] = along_x, along_y, along_z, h
        residual = (residual_ref, above_ref, below_ref)[k][x - (0, size_x, size_x + REACH)[k]]
        u_ref[x, 0:size_y, :] = residual * h[0:size_y] * (1.0 / theta)
        u_ref[x, size_y:wide_y, :] = tail_ref[x] * h[size_y:wide_y] * (1.0 / theta)
        return along_x

    sweep(REACH, faces, jnp.ones((wide_y, LANES), f32), first_ref, edge_direct)

    def smooth(x, after, edges, before):
        value, along_x, along_y, along_z = u_ref[x], x_ref[x], y_ref[x], z_ref[x]
        beside = before + along_x * u_ref[after]
        beside = beside + along_y * y_after(value) + y_before(along_y * value)
        beside = beside + along_z * z_after(value, edges) + z_before(along_z * value, edges)
        return near * value + far * (h_ref[x] * beside), along_x * value

    def direct(x, after, k, edges, before):
        value, product = smooth(x, after, edges, before)
        d_ref[x] = value + coarse_ref[k]
        return product

    outer = wide_x - 3
    sweep(2, direct, x_ref[outer] * u_ref[outer], second_ref, edge_image)

    def image_of(x, after, k, edges, carry):
        before, *found = carry
        value = d_ref[x]
        flux_x = x_ref[x] * (value - d_ref[after])
        flux_y = y_ref[x] * (value - y_after(value))
        flux_z = z_ref[x] * (value - z_after(value, edges))
        image = (flux_x - before) + (flux_y - y_before(flux_y)) + (flux_z - z_before(flux_z, edges))
        u_ref[x] = image * h_ref[x] * (1.0 / theta)
        if k == 0:
            value, image = value[0:size_y], image[0:size_y]
            direction_ref[x] = value
            parts = (residual_ref[x] * value, value * image, image)
            found = [
                total + sum(part[8 * i : 8 * i + 8] for i in range(size_y // 8))
                for total, part in zip(found, parts)
            ]
        return (flux_x, *found)

    outer = wide_x - 2
    zero = jnp.zeros((8, LANES), f32)
    _, *found = sweep(1, image_of, (x_ref[outer] * (d_ref[outer] - d_ref[outer + 1]), zero, zero, zero), third_ref)

    device = device_number(sizes)
    folded = [jnp.sum(f, axis=0, keepdims=True) for f in found]
    image_sums = place_sums(jnp.broadcast_to(folded[2], (8, LANES)), device, slabs)[0:1]
    gamma = jnp.sum(folded[0], axis=1, keepdims=True)
    curvature = jnp.sum(folded[1], axis=1, keepdims=True)
    last = jnp.where(lane8[0:1] == 0, gamma, jnp.where(lane8[0:1] == 1, curvature, 0.0))
    own_half = device // (LANES // slabs)

    def spread(i, carry):
        for h in range(halves):
            stat_ref[i, h : h + 1, :] = jnp.where(own_half == h, image_sums, 0.0)
        stat_ref[i, halves : halves + 1, :] = last
        return carry

    lax.fori_loop(0, stat_ref.shape[0], spread, 0, unroll=4)

    def second(x, after, k, edges, before):
        value, product = smooth(x, after, edges, before)
        applied_ref[x] = value[0:size_y]
        return product

    sweep(0, second, x_ref[wide_x - 1] * u_ref[wide_x - 1], fourth_ref)


def finish_kernel(
    sizes, records, halves, slabs,
    stat_ref, message_ref, other_ref, direction_ref, applied_ref, pressure_ref, preconditioned_ref,
):
    high_at, low_at, _, _ = message_rows(records, halves)
    total = lax.fori_loop(
        1, stat_ref.shape[0], lambda i, acc: acc + stat_ref[i], stat_ref[0], unroll=4
    )
    sums = [total[h : h + 1] for h in range(halves)]
    coarse = coarse_solve((message_ref, other_ref), high_at, low_at, halves, sums)
    lane8 = lane_of(8)
    own = pick(coarse, device_number(sizes), lane8 // (LANES // slabs), slabs)
    last = total[halves : halves + 1]
    alpha = last[:, 0:1] / last[:, 1:2]
    size_x, size_y, _ = direction_ref.shape
    alpha = jnp.broadcast_to(alpha, (size_y, LANES))
    own = jnp.concatenate([own] * (size_y // 8), axis=0)

    def body(x, carry):
        direction = direction_ref[x]
        pressure_ref[x] = alpha * direction
        preconditioned_ref[x] = direction - alpha * (applied_ref[x] + own)
        return carry

    lax.fori_loop(0, size_x, body, 0, unroll=2)


def cycle(value, axis, step):
    size = lax.axis_size(axis)
    return lax.ppermute(value, axis, [(i, (i + step) % size) for i in range(size)])


def exchange(value, axis, stride):
    size = lax.axis_size(axis)
    return lax.ppermute(value, axis, [(i, i ^ stride) for i in range(size)])


def doublings():
    steps = []
    for axis in ("gy", "gx", "gz"):
        strides = [1 << k for k in range(lax.axis_size(axis).bit_length() - 1)]
        steps += [(axis, stride) for stride in (strides[::-1] if axis == "gz" else strides)]
    return steps


def shards(sizes, right_side, coarse_inverse, sphere_rows, margin_block, margin_column):
    size_x, size_y, _ = right_side.shape
    slabs, subdomains = coarse_inverse.shape
    records = sphere_rows.shape[0]
    halves = subdomains // LANES
    devices = sizes[0] * sizes[1] * sizes[2]
    wide_x, wide_y = size_x + 2 * REACH, size_y + 2 * REACH
    groups = wide_x // SUBS
    planes = wide_x + groups
    f32, bf16 = jnp.float32, jnp.bfloat16
    _, _, meta_at, meta_rows = message_rows(records, halves)
    shape = jax.ShapeDtypeStruct

    def call(kernel, out_shape, operands, scratch=(), results=pltpu.VMEM, mib=8):
        outs = [results(o.shape, o.dtype) for o in out_shape]
        return pl.pallas_call(
            kernel,
            out_shape=outs,
            in_specs=[VMEM] * len(operands),
            out_specs=[VMEM] * len(outs),
            scratch_shapes=list(scratch),
            compiler_params=pltpu.CompilerParams(vmem_limit_bytes=mib << 20),
        )(*(pltpu.with_memory_space_constraint(o, pltpu.VMEM) for o in operands))

    (message,) = call(
        functools.partial(pack_kernel, sizes),
        (shape((meta_at + meta_rows, LANES), bf16),),
        (right_side, coarse_inverse, sphere_rows, margin_block.reshape(1, records), margin_column.reshape(1, records)),
        (pltpu.VMEM((8, LANES), f32),),
    )
    steps = doublings()

    def join(k, held):
        return exchange(held, *steps[k])

    held = message[None]
    received = join(0, held)
    first, last = right_side[:REACH], right_side[size_x - REACH :]
    if sizes[0] == 2:
        above = below = cycle(jnp.where(lax.axis_index("gx") == 0, last, first), "gx", 1)
    else:
        above, below = cycle(first, "gx", -1), cycle(last, "gx", 1)
    held, received, above, below = lax.optimization_barrier((held, received, above, below))
    held = jnp.concatenate([held, received], axis=0)
    received = join(1, held)
    pairs = shape((wide_x // 2, 8, LANES), f32)
    down, up = call(margin_y_kernel, (pairs, pairs), (right_side, above, below))
    after = cycle(down, "gy", -1)
    before = cycle(up, "gy", 1)
    (part,) = call(edge_own_kernel, (shape((groups, size_y, LANES), f32),), (right_side, above, below))
    held, received, after, before = lax.optimization_barrier((held, received, after, before))
    held = jnp.concatenate([held, received], axis=0)
    received = join(2, held)
    tail, edge = call(
        edge_tail_kernel,
        (shape((wide_x, 8, LANES), f32), shape((groups, wide_y, LANES), f32)),
        (part, after, before),
    )
    lower = cycle(edge, "gz", 1)
    upper = cycle(edge, "gz", -1)
    for k in range(3, len(steps)):
        held = jnp.concatenate([held, received], axis=0)
        received = join(k, held)

    half = devices // 2
    depth = min(half, 16) * LANES
    rows_all = 16 * pl.cdiv(groups * wide_y, 16)
    field = pltpu.VMEM((planes, wide_y, LANES), f32)
    margin = pltpu.VMEM((groups, wide_y, LANES), f32)
    kinds = pltpu.VMEM((5, wide_y, LANES), f32)
    block = shape((size_x, size_y, LANES), f32)
    direction, applied, stats = call(
        functools.partial(main_kernel, sizes, records, halves, slabs, size_x, size_y),
        (block, block, shape((devices, halves + 1, LANES), f32)),
        (held, received, right_side, above, below, tail, edge, lower, upper),
        (
            pltpu.VMEM((3, devices, LANES), f32),
            pltpu.VMEM((half, LANES), f32),
            pltpu.VMEM((2, LANES, LANES), f32),
            pltpu.VMEM((rows_all, depth), bf16),
            pltpu.VMEM((depth, (SUBS + 1) * LANES), bf16),
            pltpu.VMEM((rows_all, (SUBS + 1) * LANES), f32),
            field, field, field, field, field, field, field, kinds, kinds,
            margin, margin, margin, margin,
        ),
        mib=28,
    )
    stats = lax.all_to_all(stats, AXES, 0, 0, tiled=True)
    return call(
        functools.partial(finish_kernel, sizes, records, halves, slabs),
        (block, block),
        (stats, held, received, direction, applied),
        results=shape,
    )


def solution(mesh):
    placed = (
        P("gx", "gy", "gz"),
        P(("gx", "gy", "gz"), None),
        P(("gx", "gy", "gz"), None),
        P(("gx", "gy", "gz"), None),
        P(("gx", "gy", "gz")),
    )
    sizes = tuple(mesh.shape[axis] for axis in AXES)

    def body(*operands):
        return shards(sizes, *operands)

    return jax.shard_map(
        body,
        mesh=mesh,
        in_specs=placed,
        out_specs=(P("gx", "gy", "gz"), P("gx", "gy", "gz")),
        check_vma=False,
    )
```

```python
import functools

import jax
import jax.numpy as jnp
from jax import lax
from jax.experimental import pallas as pl
from jax.experimental.pallas import tpu as pltpu
from jax.sharding import PartitionSpec as P


bound_low = 0.1
bound_high = 2.0
theta = 0.5 * (bound_high + bound_low)
delta = 0.5 * (bound_high - bound_low)
weight_first = delta / theta
weight_second = 1.0 / (2.0 * theta / delta - weight_first)
far = 2.0 * weight_second / delta
near = 1.0 + weight_second * weight_first + far * (theta - 1.0)

AXES = ("gx", "gy", "gz")
LANES = 128
REACH = 4
DEEP = 3
SUBS = 8
SLOT = 64
EXACT = lax.Precision.HIGHEST
VMEM = pl.BlockSpec(memory_space=pltpu.VMEM)


def lane_of(rows):
    return lax.broadcasted_iota(jnp.int32, (rows, LANES), 1)


def row_of(rows):
    return lax.broadcasted_iota(jnp.int32, (rows, LANES), 0)


def by_parity(axis, one, two):
    even = lax.axis_index(axis) % 2 == 0
    return jnp.where(even, one, two), jnp.where(even, two, one)


def message_rows(records, halves):
    meta = 16 * pl.cdiv(3 + 3 * halves, 16)
    return records, records + 8 * halves, records + 16 * halves, meta


def place_sums(total, device, slabs):
    width = LANES // slabs
    base = lax.rem(device, width) * slabs
    source = lax.broadcasted_iota(jnp.int32, (LANES, LANES), 0)
    target = lax.broadcasted_iota(jnp.int32, (LANES, LANES), 1)
    first = (target - base) * width
    chosen = (source >= first) & (source < first + width) & (target >= base) & (target < base + slabs)
    return jnp.dot(total, chosen.astype(jnp.float32), precision=EXACT, preferred_element_type=jnp.float32)


def device_number(sizes):
    return (lax.axis_index("gx") * sizes[1] + lax.axis_index("gy")) * sizes[2] + lax.axis_index("gz")


def pack_kernel(sizes, residual_ref, inverse_ref, rows_ref, block_ref, column_ref, out_ref, *rest):
    *margin_refs, index_ref = rest
    size_x, size_y, _ = residual_ref.shape
    slabs, subdomains = inverse_ref.shape
    records = rows_ref.shape[0]
    halves = subdomains // LANES
    high_at, low_at, meta_at, meta_rows = message_rows(records, halves)
    out_ref[0:records, :] = rows_ref[...]
    own = (slice(0, DEEP), slice(size_x - DEEP, size_x))
    if len(margin_refs) == 1:
        is_first = lax.axis_index("gx") == 0
        margin_refs[0][...] = jnp.where(is_first, residual_ref[own[1]], residual_ref[own[0]])
    else:
        margin_refs[0][...], margin_refs[1][...] = residual_ref[own[0]], residual_ref[own[1]]
    whole = jnp.concatenate([inverse_ref[:, h * LANES : (h + 1) * LANES] for h in range(halves)], axis=0)
    high = whole.astype(jnp.bfloat16)
    out_ref[high_at : high_at + 8 * halves, :] = high
    out_ref[low_at : low_at + 8 * halves, :] = (whole - high.astype(jnp.float32)).astype(jnp.bfloat16)

    index_ref[...] = jnp.zeros_like(index_ref)
    index_ref[0:1, 0:records] = block_ref[...].astype(jnp.float32) + 1.0
    column = column_ref[...].astype(jnp.float32)
    plane = jnp.floor((column + 0.5) * (1.0 / size_y))
    index_ref[1:2, 0:records] = plane + (lax.axis_index("gx") * size_x).astype(jnp.float32)
    index_ref[2:3, 0:records] = column - plane * size_y

    total = lax.fori_loop(
        1, size_x, lambda i, acc: acc + residual_ref[i], residual_ref[0], unroll=4
    )
    total = jnp.broadcast_to(jnp.sum(total, axis=0, keepdims=True), (8, LANES))
    device = device_number(sizes)
    sums = place_sums(total, device, slabs)[0:1]
    high = sums.astype(jnp.bfloat16).astype(jnp.float32)
    middle = (sums - high).astype(jnp.bfloat16).astype(jnp.float32)
    low = sums - high - middle
    half = device // (LANES // slabs)
    row = row_of(meta_rows)
    meta = jnp.where(row == 0, index_ref[0:1, :], 0.0)
    meta = jnp.where(row == 1, index_ref[1:2, :], meta)
    meta = jnp.where(row == 2, index_ref[2:3, :], meta)
    meta = jnp.where(row == 3 + half, high, meta)
    meta = jnp.where(row == 3 + halves + half, middle, meta)
    meta = jnp.where(row == 3 + 2 * halves + half, low, meta)
    out_ref[meta_at : meta_at + meta_rows, :] = meta.astype(jnp.bfloat16)


def beside(i, above_ref, below_ref):
    return above_ref.at[min(i, DEEP - 1)] if i < REACH else below_ref.at[max(i - 2 * REACH + DEEP, 0)]


def margin_y_kernel(residual_ref, above_ref, below_ref, within_ref, across_ref):
    size_x, size_y, _ = residual_ref.shape
    row = row_of(8)

    def plane(x, at):
        if x < size_x:
            return residual_ref[x, pl.ds(at, 8), :]
        x -= size_x
        return beside(x, above_ref, below_ref)[pl.ds(at, 8), :]

    for pair in range((size_x + 2 * REACH) // 2):
        low = [plane(2 * pair + k, 0) for k in range(2)]
        high = [plane(2 * pair + k, size_y - 8) for k in range(2)]
        down = jnp.where(row < 4, low[0], pltpu.roll(low[1], 4, 0))
        up = jnp.where(row < 4, pltpu.roll(high[1], 4, 0), high[0])
        within_ref[pair], across_ref[pair] = by_parity("gy", up, down)


def edge_group(values):
    rows = values[0].shape[0]
    place, sub_of = lane_of(rows) % 16, lane_of(rows) // 16
    edge = jnp.zeros((rows, LANES), jnp.float32)
    for sub, value in enumerate(values):
        first = pltpu.roll(value, (sub * 16 + 4) % LANES, 1)
        last = pltpu.roll(value, (sub * 16 + 12) % LANES, 1)
        edge = jnp.where((sub_of == sub) & (place >= 4) & (place < 8), first, edge)
        edge = jnp.where((sub_of == sub) & (place >= 8) & (place < 12), last, edge)
    return edge


def edge_own_kernel(residual_ref, above_ref, below_ref, edge_ref):
    groups = edge_ref.shape[0]

    def group(g, carry):
        edge_ref[g] = edge_group([residual_ref[g * SUBS + sub] for sub in range(SUBS)])
        return carry

    lax.fori_loop(0, groups - 1, group, 0)
    edge_ref[groups - 1] = edge_group([beside(i, above_ref, below_ref)[...] for i in range(2 * REACH)])


def edge_tail_kernel(part_ref, within_ref, across_ref, tail_ref, edge_ref, down_ref, up_ref):
    groups, size_y, _ = part_ref.shape
    row = row_of(8)
    place = lane_of(size_y + 2 * REACH) % 16
    down = up = jnp.zeros(down_ref.shape, jnp.float32)
    for g in range(groups):
        tails = []
        for x in range(g * SUBS, g * SUBS + SUBS):
            after, before = by_parity("gy", within_ref[x // 2], across_ref[x // 2])
            if x % 2:
                after, before = pltpu.roll(after, 4, 0), pltpu.roll(before, 4, 0)
            tails.append(jnp.where(row < 4, after, before))
            tail_ref[x] = tails[-1]
        edge_ref[g, 0:size_y, :] = part_ref[g]
        edge_ref[g, size_y:, :] = edge_group(tails)
        here = (place >= DEEP * g) & (place < DEEP * (g + 1))
        down = jnp.where(here, pltpu.roll(edge_ref[g], (DEEP * g - 4) % LANES, 1), down)
        up = jnp.where(here, pltpu.roll(edge_ref[g], (DEEP * g + DEEP - 12) % LANES, 1), up)
    down_ref[...], up_ref[...] = down, up


def coarse_solve(message_refs, high_at, low_at, halves, sums):
    def body(message_ref, i, total):
        high = message_ref[i, high_at : high_at + 8 * halves, :].astype(jnp.float32)
        low = message_ref[i, low_at : low_at + 8 * halves, :].astype(jnp.float32)
        rows = high + low
        tiles = [rows[8 * h : 8 * h + 8] for h in range(halves)]
        inner = sum(tiles[h] * sums[h] for h in range(halves))
        inner = jnp.sum(inner, axis=1, keepdims=True)
        return tuple(total[h] + inner * tiles[h] for h in range(halves))

    zero = jnp.zeros((8, LANES), jnp.float32)
    total = (zero,) * halves
    for ref in message_refs:
        total = lax.fori_loop(0, ref.shape[0], functools.partial(body, ref), total, unroll=8)
    return [jnp.broadcast_to(jnp.sum(t, axis=0, keepdims=True), (8, LANES)) for t in total]


def pick(values, device, slab, slabs):
    per_half = LANES // slabs
    half = device // per_half
    chosen = values[0]
    for h in range(1, len(values)):
        chosen = jnp.where(half == h, values[h], chosen)
    index = lax.rem(device, per_half) * slabs + slab
    return jnp.take_along_axis(chosen, index, axis=1)


def y_after(value):
    return pltpu.roll(value, value.shape[0] - 1, 0)


def y_before(value):
    return pltpu.roll(value, 1, 0)


def z_after(value, edges):
    return jnp.where(lane_of(value.shape[0]) == LANES - 1, edges, pltpu.roll(value, LANES - 1, 1))


def z_before(value, edges):
    return jnp.where(lane_of(value.shape[0]) == 0, edges, pltpu.roll(value, 1, 1))


def smooth(refs, x, after, edges, before):
    u_ref, x_ref, y_ref, z_ref, h_ref = refs
    value, along_x, along_y, along_z = u_ref[x], x_ref[x], y_ref[x], z_ref[x]
    total = before + along_x * u_ref[after]
    total = total + along_y * y_after(value) + y_before(along_y * value)
    total = total + along_z * z_after(value, edges) + z_before(along_z * value, edges)
    return near * value + far * (h_ref[x] * total), along_x * value


def smooth_again(u_ref, x_ref, y_ref, z_ref, h_ref, joined_ref, applied_ref):
    size_x, size_y, _ = applied_ref.shape
    outer = size_x + 2 * REACH - 1

    def group(g, before):
        for sub in range(SUBS):
            x = g * SUBS + sub
            edges = pltpu.roll(joined_ref[g], 115 - 16 * sub, 1)
            value, before = smooth((u_ref, x_ref, y_ref, z_ref, h_ref), x, x + 1, edges, before)
            applied_ref[x] = value[0:size_y]
        return before

    lax.fori_loop(0, size_x // SUBS, group, x_ref[outer] * u_ref[outer])


def main_kernel(
    sizes, records, halves, slabs, size_x, size_y,
    message_ref, other_ref, residual_ref, above_ref, below_ref, tail_ref, edge_ref, lower_ref, upper_ref,
    direction_ref, applied_ref, stat_ref,
    key_ref, code_ref, turned_ref, left_ref, right_ref, added_ref,
    density_ref, x_ref, y_ref, z_ref, h_ref, u_ref, d_ref, inside_ref, coarse_ref,
    first_ref, second_ref, third_ref, fourth_ref,
):
    n_gx, n_gy, n_gz = sizes
    gx, gy, gz = (lax.axis_index(a) for a in AXES)
    half = message_ref.shape[0]
    wide_x, wide_y = size_x + 2 * REACH, size_y + 2 * REACH
    groups = wide_x // SUBS
    high_at, low_at, meta_at, meta_rows = message_rows(records, halves)
    f32, bf16 = jnp.float32, jnp.bfloat16
    lane = lane_of(wide_y)
    row = row_of(wide_y)
    place = lane % 16

    def roll(value, shift, axis):
        return pltpu.roll(value, shift, axis)

    def read_meta(i, total):
        for j, ref in enumerate((message_ref, other_ref)):
            tile = ref[i, meta_at : meta_at + meta_rows, :].astype(f32)
            for k in range(3):
                key_ref[k, pl.ds(i + j * half, 1), :] = tile[k : k + 1]
            total = total + tile
        return total

    total = lax.fori_loop(0, half, read_meta, jnp.zeros((meta_rows, LANES), f32), unroll=4)
    sums = [
        total[3 + h : 4 + h] + total[3 + halves + h : 4 + halves + h] + total[3 + 2 * halves + h : 4 + 2 * halves + h]
        for h in range(halves)
    ]
    coarse = coarse_solve((message_ref, other_ref), high_at, low_at, halves, sums)

    def there(ix, iy, iz):
        ok = (ix >= 0) & (ix < n_gx) & (iy >= 0) & (iy < n_gy) & (iz >= 0) & (iz < n_gz)
        return ok.astype(f32), jnp.where(ok, (ix * n_gy + iy) * n_gz + iz, 0)

    lane8 = lane_of(8)
    row8 = row_of(8)
    place8 = lane8 % 16
    constant = lambda k: jnp.full((8, LANES), k, jnp.int32)

    def main_values(ix, iy):
        ok, device = there(ix, iy, gz)
        return jnp.full((8, LANES), ok, f32), ok * pick(coarse, device, lane8 // (LANES // slabs), slabs)

    def edge_values(ix, iy):
        parts = []
        for iz, slab in ((gz - 1, slabs - 1), (gz, 0), (gz, slabs - 1), (gz + 1, 0)):
            ok, device = there(ix, iy, iz)
            parts.append((jnp.full((8, LANES), ok, f32), ok * pick(coarse, device, constant(slab), slabs)))
        out = []
        for k in range(2):
            value = jnp.where(place8 < 4, parts[0][k], parts[1][k])
            value = jnp.where(place8 >= 8, parts[2][k], value)
            out.append(jnp.where(place8 >= 12, parts[3][k], value))
        return out

    def fill(kind, values_at):
        own, after, before = values_at(gy), values_at(gy + 1), values_at(gy - 1)
        for k, ref in enumerate((inside_ref, coarse_ref)):
            ref[kind, 0:size_y, :] = jnp.concatenate([own[k]] * (size_y // 8), axis=0)
            ref[kind, size_y:wide_y, :] = jnp.where(row8 < 4, after[k], before[k])

    def beside_x(iy):
        above, below = edge_values(gx + 1, iy), edge_values(gx - 1, iy)
        return [jnp.where(lane8 < 4 * 16, a, b) for a, b in zip(above, below)]

    fill(0, lambda iy: main_values(gx, iy))
    fill(1, lambda iy: main_values(gx + 1, iy))
    fill(2, lambda iy: main_values(gx - 1, iy))
    fill(3, lambda iy: edge_values(gx, iy))
    fill(4, beside_x)

    block, plane, line = (key_ref[k, 0:half, :] + roll(key_ref[k, half : 2 * half, :], SLOT, 1) for k in range(3))
    valid = block > 0.5
    block = block - 1.0
    block_y = jnp.floor((block + 0.5) * (1.0 / n_gz))
    side = block - block_y * n_gz - gz.astype(f32)
    at_x = plane - (gx * size_x).astype(f32)
    at_y = (block_y - gy.astype(f32)) * size_y + line
    valid = valid & (at_x >= -REACH) & (at_x < size_x + REACH) & (at_y >= -REACH) & (at_y < size_y + REACH)
    at_x = jnp.where(at_x < 0, at_x + wide_x, at_x)
    at_y = jnp.where(at_y < 0, at_y + wide_y, at_y)
    at_group = jnp.floor((at_x + 0.5) * (1.0 / SUBS))
    at_sub = at_x - at_group * SUBS
    code_ref[...] = jnp.where(valid, at_group * wide_y + at_y, -1.0)
    turned_ref[...] = jnp.full(turned_ref.shape, -1.0, f32)
    turned_ref[0, 0:half, :] = jnp.where(side == 0, at_sub, -1.0)
    turned_ref[1, 0:half, :] = jnp.where((side >= -1) & (side <= 1), at_sub + SUBS * (side + 1), -1.0)
    turned_ref[0] = turned_ref[0].T
    turned_ref[1] = turned_ref[1].T

    chunk = min(half, 16)
    rows_all = left_ref.shape[0]
    row_number = lax.broadcasted_iota(jnp.int32, (rows_all, LANES), 0).astype(f32)
    source = lax.broadcasted_iota(jnp.int32, (LANES, LANES), 0)
    target = lax.broadcasted_iota(jnp.int32, (LANES, LANES), 1)
    wanted = jnp.where(target % 8 < 4, target % 4 + (LANES - 4), target % 4)
    chooser = (source == wanted).astype(bf16)
    kind = jnp.where(target % 16 < 4, 0, jnp.where(target % 16 < 12, 1, 2))
    edge_code = (target // 16 + SUBS * kind).astype(f32)

    for c in range(half // chunk):
        def build(q, carry, c=c):
            p = q + c * chunk
            at = pl.ds(pl.multiple_of(q * LANES, LANES), LANES)
            code = code_ref[pl.ds(p, 1), :]
            left_ref[:, at] = jnp.where(row_number == code, 1.0, 0.0).astype(bf16)
            rows = jnp.concatenate([message_ref[p, 0:SLOT, :], other_ref[p, 0:SLOT, :]], axis=0)
            turn = lax.rem(LANES - p, LANES)
            key = jnp.broadcast_to(roll(turned_ref[0], turn, 1)[:, 0:1], (LANES, LANES))
            edge_key = jnp.broadcast_to(roll(turned_ref[1], turn, 1)[:, 0:1], (LANES, LANES))
            key = key.astype(bf16)
            for sub in range(SUBS):
                chosen = jnp.where(key == sub, rows, jnp.zeros_like(rows))
                right_ref[at, sub * LANES : (sub + 1) * LANES] = chosen
            edges = jnp.dot(rows, chooser, preferred_element_type=f32)
            right_ref[at, SUBS * LANES :] = jnp.where(edge_key == edge_code, edges, 0.0).astype(bf16)
            return carry

        lax.fori_loop(0, chunk, build, 0, unroll=4)
        for n in range(0, SUBS + 1, 2):
            columns = slice(n * LANES, min(n + 2, SUBS + 1) * LANES)
            product = jnp.dot(left_ref[...], right_ref[:, columns], preferred_element_type=f32)
            added_ref[:, columns] = product if c == 0 else added_ref[:, columns] + product

    for g in range(groups):
        lines = slice(g * wide_y, (g + 1) * wide_y)
        for sub in range(SUBS):
            x = g * SUBS + sub
            k = 0 if x < size_x else 1 if x < size_x + REACH else 2
            density_ref[x] = inside_ref[k] + added_ref[lines, sub * LANES : (sub + 1) * LANES]
        k = 3 if g < groups - 1 else 4
        density_ref[wide_x + g] = inside_ref[k] + added_ref[lines, SUBS * LANES :]

    def joined(after, before):
        return jnp.where(place == 13, roll(before, 10, 1), after)

    def edge_x_after(value, other):
        return jnp.where(lane >= LANES - 16, roll(other, LANES - 16, 1), roll(value, LANES - 16, 1))

    def edge_x_before(value, other):
        return jnp.where(lane < 16, roll(other, 16, 1), roll(value, 16, 1))

    def sweep(reach, body, carry, joined_ref, beside=None):
        def turned(g, sub):
            return roll(joined_ref[g], 115 - 16 * sub, 1)

        for x in range(-reach, 0):
            after = wide_x + x + 1 if x < -1 else 0
            carry = body(wide_x + x, after, 2, turned(groups - 1, SUBS + x), carry)

        def group(g, carry):
            if beside:
                beside(g, jnp.where(g == 0, groups - 1, g - 1), g + 1, 3)
            for sub in range(SUBS):
                x = g * SUBS + sub
                carry = body(x, x + 1, 0, turned(g, sub), carry)
            return carry

        carry = lax.fori_loop(0, groups - 1, group, carry)
        if beside:
            beside(groups - 1, groups - 2, 0, 4)
        for x in range(reach):
            carry = body(size_x + x, size_x + x + 1, 1, turned(groups - 1, x), carry)
        return carry

    def beta(one, two):
        return 2.0 / jnp.maximum(one + two, 0.5)

    for g in range(groups):
        j = wide_x + g
        value = density_ref[j]
        x_ref[j] = beta(value, edge_x_after(value, density_ref[wide_x + (g + 1) % groups]))
        y_ref[j] = beta(value, y_after(value))
        z_ref[j] = beta(value, roll(value, LANES - 1, 1))

    for g in range(groups):
        j = wide_x + g
        before_x = edge_x_before(x_ref[j], x_ref[wide_x + (g - 1) % groups])
        diagonal = x_ref[j] + before_x + y_ref[j] + y_before(y_ref[j]) + z_ref[j] + roll(z_ref[j], 1, 1)
        h = inside_ref[3 if g < groups - 1 else 4] / diagonal
        h_ref[j] = h
        residual = edge_ref[g]
        lower = roll(lower_ref[...], (4 - DEEP - DEEP * g) % LANES, 1)
        upper = roll(upper_ref[...], 12 - DEEP * g, 1)
        residual = jnp.where((place >= 4 - DEEP) & (place < 4), lower, residual)
        residual = jnp.where((place >= 12) & (place < 12 + DEEP), upper, residual)
        u_ref[j] = residual * h * (1.0 / theta)
        first_ref[g] = joined(density_ref[j], z_ref[j])

    def edge_direct(g, before_g, after_g, k):
        j, before_j, after_j = wide_x + g, wide_x + before_g, wide_x + after_g
        value, along_x, along_y, along_z = u_ref[j], x_ref[j], y_ref[j], z_ref[j]
        product_z = along_z * value
        beside = along_x * edge_x_after(value, u_ref[after_j])
        beside = beside + edge_x_before(along_x * value, x_ref[before_j] * u_ref[before_j])
        beside = beside + along_y * y_after(value) + y_before(along_y * value)
        beside = beside + along_z * roll(value, LANES - 1, 1) + roll(product_z, 1, 1)
        d_ref[j] = near * value + far * (h_ref[j] * beside) + coarse_ref[k]
        second_ref[g] = joined(value, product_z)

    def edge_image(g, before_g, after_g, k):
        j, before_j, after_j = wide_x + g, wide_x + before_g, wide_x + after_g
        value, before = d_ref[j], d_ref[before_j]
        flux_x = x_ref[j] * (value - edge_x_after(value, d_ref[after_j]))
        flux_y = y_ref[j] * (value - y_after(value))
        flux_z = z_ref[j] * (value - roll(value, LANES - 1, 1))
        image = flux_x + edge_x_before(x_ref[j], x_ref[before_j]) * (value - edge_x_before(value, before))
        image = image + (flux_y - y_before(flux_y)) + (flux_z - roll(flux_z, 1, 1))
        image = image * h_ref[j] * (1.0 / theta)
        third_ref[g] = joined(value, flux_z)
        fourth_ref[g] = joined(image, z_ref[j] * image)

    def faces(x, after, k, edges, before):
        value = density_ref[x]
        sum_x, sum_y, sum_z = (
            jnp.maximum(value + other, 0.5)
            for other in (density_ref[after], y_after(value), z_after(value, edges))
        )
        both = sum_x * sum_y
        common = 2.0 / (both * sum_z)
        along_z = common * both
        common = common * sum_z
        along_x = common * sum_y
        along_y = common * sum_x
        diagonal = before + along_x + along_y + y_before(along_y) + along_z + z_before(along_z, edges)
        h = inside_ref[k] / diagonal
        x_ref[x], y_ref[x], z_ref[x], h_ref[x] = along_x, along_y, along_z, h
        residual = residual_ref[x] if k == 0 else beside(x - size_x, above_ref, below_ref)[...]
        u_ref[x, 0:size_y, :] = residual * h[0:size_y] * (1.0 / theta)
        u_ref[x, size_y:wide_y, :] = tail_ref[x] * h[size_y:wide_y] * (1.0 / theta)
        return along_x

    sweep(REACH, faces, jnp.ones((wide_y, LANES), f32), first_ref, edge_direct)

    def direct(x, after, k, edges, before):
        value, product = smooth((u_ref, x_ref, y_ref, z_ref, h_ref), x, after, edges, before)
        d_ref[x] = value + coarse_ref[k]
        return product

    outer = wide_x - 3
    sweep(2, direct, x_ref[outer] * u_ref[outer], second_ref, edge_image)

    def image_of(x, after, k, edges, carry):
        before, *found = carry
        value = d_ref[x]
        flux_x = x_ref[x] * (value - d_ref[after])
        flux_y = y_ref[x] * (value - y_after(value))
        flux_z = z_ref[x] * (value - z_after(value, edges))
        image = (flux_x - before) + (flux_y - y_before(flux_y)) + (flux_z - z_before(flux_z, edges))
        u_ref[x] = image * h_ref[x] * (1.0 / theta)
        if k == 0:
            value, image = value[0:size_y], image[0:size_y]
            direction_ref[x] = value
            parts = (residual_ref[x] * value, value * image, image)
            found = [
                total + sum(part[8 * i : 8 * i + 8] for i in range(size_y // 8))
                for total, part in zip(found, parts)
            ]
        return (flux_x, *found)

    outer = wide_x - 2
    zero = jnp.zeros((8, LANES), f32)
    _, *found = sweep(1, image_of, (x_ref[outer] * (d_ref[outer] - d_ref[outer + 1]), zero, zero, zero), third_ref)

    device = device_number(sizes)
    folded = [jnp.sum(f, axis=0, keepdims=True) for f in found]
    image_sums = place_sums(jnp.broadcast_to(folded[2], (8, LANES)), device, slabs)[0:1]
    gamma = jnp.sum(folded[0], axis=1, keepdims=True)
    curvature = jnp.sum(folded[1], axis=1, keepdims=True)
    last = jnp.where(lane8[0:1] == 0, gamma, jnp.where(lane8[0:1] == 1, curvature, 0.0))
    own_half = device // (LANES // slabs)

    def spread(i, carry):
        for h in range(halves):
            stat_ref[i, h : h + 1, :] = jnp.where(own_half == h, image_sums, 0.0)
        stat_ref[i, halves : halves + 1, :] = last
        return carry

    lax.fori_loop(0, stat_ref.shape[0], spread, 0, unroll=4)

    smooth_again(u_ref, x_ref, y_ref, z_ref, h_ref, fourth_ref, applied_ref)


def finish_kernel(
    sizes, records, halves, slabs,
    stat_ref, message_ref, other_ref, direction_ref, applied_ref, pressure_ref, preconditioned_ref,
):
    high_at, low_at, _, _ = message_rows(records, halves)
    total = lax.fori_loop(
        1, stat_ref.shape[0], lambda i, acc: acc + stat_ref[i], stat_ref[0], unroll=4
    )
    sums = [total[h : h + 1] for h in range(halves)]
    coarse = coarse_solve((message_ref, other_ref), high_at, low_at, halves, sums)
    lane8 = lane_of(8)
    own = pick(coarse, device_number(sizes), lane8 // (LANES // slabs), slabs)
    last = total[halves : halves + 1]
    alpha = last[:, 0:1] / last[:, 1:2]
    size_x, size_y, _ = direction_ref.shape
    alpha = jnp.broadcast_to(alpha, (size_y, LANES))
    own = jnp.concatenate([own] * (size_y // 8), axis=0)

    def body(x, carry):
        direction = direction_ref[x]
        pressure_ref[x] = alpha * direction
        preconditioned_ref[x] = direction - alpha * (applied_ref[x] + own)
        return carry

    lax.fori_loop(0, size_x, body, 0, unroll=2)


def cycle(value, axis, step):
    size = lax.axis_size(axis)
    return lax.ppermute(value, axis, [(i, (i + step) % size) for i in range(size)])


def swap_within(value, axis):
    return lax.ppermute(value, axis, [(i, i ^ 1) for i in range(lax.axis_size(axis))])


def swap_across(value, axis):
    size = lax.axis_size(axis)
    to = {i: i if i in (0, size - 1) else i + 1 if i % 2 else i - 1 for i in range(size)}
    return lax.ppermute(value, axis, sorted(to.items()))


def exchange(value, axis, stride):
    size = lax.axis_size(axis)
    return lax.ppermute(value, axis, [(i, i ^ stride) for i in range(size)])


def doublings():
    steps = []
    for axis in ("gy", "gx", "gz"):
        strides = [1 << k for k in range(lax.axis_size(axis).bit_length() - 1)]
        steps += [(axis, stride) for stride in strides[::-1]]
    return steps


def shards(sizes, right_side, coarse_inverse, sphere_rows, margin_block, margin_column):
    size_x, size_y, _ = right_side.shape
    slabs, subdomains = coarse_inverse.shape
    records = sphere_rows.shape[0]
    halves = subdomains // LANES
    devices = sizes[0] * sizes[1] * sizes[2]
    wide_x, wide_y = size_x + 2 * REACH, size_y + 2 * REACH
    groups = wide_x // SUBS
    planes = wide_x + groups
    f32, bf16 = jnp.float32, jnp.bfloat16
    _, _, meta_at, meta_rows = message_rows(records, halves)
    shape = jax.ShapeDtypeStruct

    def call(kernel, out_shape, operands, scratch=(), results=pltpu.VMEM, mib=8, left=()):
        outs = [results(o.shape, o.dtype) for o in out_shape]
        return pl.pallas_call(
            kernel,
            out_shape=outs,
            in_specs=[VMEM] * len(operands),
            out_specs=[VMEM] * len(outs),
            scratch_shapes=list(scratch),
            compiler_params=pltpu.CompilerParams(vmem_limit_bytes=mib << 20),
        )(*(pltpu.with_memory_space_constraint(o, pltpu.HBM if i in left else pltpu.VMEM) for i, o in enumerate(operands)))

    planes_sent = shape((DEEP, size_y, LANES), f32)
    swap = sizes[0] == 2
    message, *margin = call(
        functools.partial(pack_kernel, sizes),
        (shape((meta_at + meta_rows, LANES), bf16),) + (planes_sent,) * (1 if swap else 2),
        (right_side, coarse_inverse, sphere_rows, margin_block.reshape(1, records), margin_column.reshape(1, records)),
        (pltpu.VMEM((8, LANES), f32),),
        left=(1, 2, 3, 4),
    )
    steps = doublings()

    def join(k, held):
        return exchange(held, *steps[k])

    held = message[None]
    received = join(0, held)
    if swap:
        above = below = cycle(margin[0], "gx", 1)
    else:
        above, below = cycle(margin[0], "gx", -1), cycle(margin[1], "gx", 1)
    held, received, above, below = lax.optimization_barrier((held, received, above, below))
    held = jnp.concatenate([held, received], axis=0)
    received = join(1, held)
    pairs = shape((wide_x // 2, 8, LANES), f32)
    within, across = call(margin_y_kernel, (pairs, pairs), (right_side, above, below))
    within = swap_within(within, "gy")
    across = swap_across(across, "gy")
    (part,) = call(edge_own_kernel, (shape((groups, size_y, LANES), f32),), (right_side, above, below))
    held = jnp.concatenate([held, received], axis=0)
    received = join(2, held)
    line = shape((wide_y, LANES), f32)
    tail, edge, down, up = call(
        edge_tail_kernel,
        (shape((wide_x, 8, LANES), f32), shape((groups, wide_y, LANES), f32), line, line),
        (part, within, across),
    )
    lower = cycle(up, "gz", 1)
    upper = cycle(down, "gz", -1)
    for k in range(3, len(steps)):
        held = jnp.concatenate([held, received], axis=0)
        received = join(k, held)

    half = devices // 2
    depth = min(half, 16) * LANES
    rows_all = 16 * pl.cdiv(groups * wide_y, 16)
    field = pltpu.VMEM((planes, wide_y, LANES), f32)
    edges = (groups, wide_y, LANES)
    margin = pltpu.VMEM(edges, f32)
    kinds = pltpu.VMEM((5, wide_y, LANES), f32)
    block = shape((size_x, size_y, LANES), f32)
    direction, applied, stats = call(
        functools.partial(main_kernel, sizes, records, halves, slabs, size_x, size_y),
        (block, block, shape((devices, halves + 1, LANES), f32)),
        (held, received, right_side, above, below, tail, edge, lower, upper),
        (
            pltpu.VMEM((3, devices, LANES), f32),
            pltpu.VMEM((half, LANES), f32),
            pltpu.VMEM((2, LANES, LANES), f32),
            pltpu.VMEM((rows_all, depth), bf16),
            pltpu.VMEM((depth, (SUBS + 1) * LANES), bf16),
            pltpu.VMEM((rows_all, (SUBS + 1) * LANES), f32),
            field, field, field, field, field, field, field, kinds, kinds, margin, margin, margin, margin,
        ),
        mib=28,
    )
    stats = lax.all_to_all(stats, AXES, 0, 0, tiled=True)
    return call(
        functools.partial(finish_kernel, sizes, records, halves, slabs),
        (block, block),
        (stats, held, received, direction, applied),
        results=shape,
    )


def solution(mesh):
    placed = (
        P("gx", "gy", "gz"),
        P(("gx", "gy", "gz"), None),
        P(("gx", "gy", "gz"), None),
        P(("gx", "gy", "gz"), None),
        P(("gx", "gy", "gz")),
    )
    sizes = tuple(mesh.shape[axis] for axis in AXES)

    def body(*operands):
        return shards(sizes, *operands)

    return jax.shard_map(
        body,
        mesh=mesh,
        in_specs=placed,
        out_specs=(P("gx", "gy", "gz"), P("gx", "gy", "gz")),
        check_vma=False,
    )
```

```python
import functools

import jax
import jax.numpy as jnp
from jax import lax
from jax.experimental import pallas as pl
from jax.experimental.pallas import tpu as pltpu
from jax.sharding import PartitionSpec as P


bound_low = 0.1
bound_high = 2.0
theta = 0.5 * (bound_high + bound_low)
delta = 0.5 * (bound_high - bound_low)
weight_first = delta / theta
weight_second = 1.0 / (2.0 * theta / delta - weight_first)
far = 2.0 * weight_second / delta
near = 1.0 + weight_second * weight_first + far * (theta - 1.0)

AXES = ("gx", "gy", "gz")
LANES = 128
REACH = 4
DEEP = 3
SUBS = 8
SLOT = 64
EXACT = lax.Precision.HIGHEST
VMEM = pl.BlockSpec(memory_space=pltpu.VMEM)


def lane_of(rows):
    return lax.broadcasted_iota(jnp.int32, (rows, LANES), 1)


def row_of(rows):
    return lax.broadcasted_iota(jnp.int32, (rows, LANES), 0)


def by_parity(axis, one, two):
    even = lax.axis_index(axis) % 2 == 0
    return jnp.where(even, one, two), jnp.where(even, two, one)


def message_rows(records, halves):
    meta = 16 * pl.cdiv(3 + 3 * halves, 16)
    return records, records + 8 * halves, records + 16 * halves, meta


def place_sums(total, device, slabs):
    width = LANES // slabs
    base = lax.rem(device, width) * slabs
    source = lax.broadcasted_iota(jnp.int32, (LANES, LANES), 0)
    target = lax.broadcasted_iota(jnp.int32, (LANES, LANES), 1)
    first = (target - base) * width
    chosen = (source >= first) & (source < first + width) & (target >= base) & (target < base + slabs)
    return jnp.dot(total, chosen.astype(jnp.float32), precision=EXACT, preferred_element_type=jnp.float32)


def device_number(sizes):
    return (lax.axis_index("gx") * sizes[1] + lax.axis_index("gy")) * sizes[2] + lax.axis_index("gz")


def pack_kernel(sizes, residual_ref, inverse_ref, rows_ref, block_ref, column_ref, out_ref, *rest):
    *margin_refs, index_ref = rest
    size_x, size_y, _ = residual_ref.shape
    slabs, subdomains = inverse_ref.shape
    records = rows_ref.shape[0]
    halves = subdomains // LANES
    high_at, low_at, meta_at, meta_rows = message_rows(records, halves)
    out_ref[0:records, :] = rows_ref[...]
    own = (slice(0, DEEP), slice(size_x - DEEP, size_x))
    if len(margin_refs) == 1:
        is_first = lax.axis_index("gx") == 0
        margin_refs[0][...] = jnp.where(is_first, residual_ref[own[1]], residual_ref[own[0]])
    else:
        margin_refs[0][...], margin_refs[1][...] = residual_ref[own[0]], residual_ref[own[1]]
    whole = jnp.concatenate([inverse_ref[:, h * LANES : (h + 1) * LANES] for h in range(halves)], axis=0)
    high = whole.astype(jnp.bfloat16)
    out_ref[high_at : high_at + 8 * halves, :] = high
    out_ref[low_at : low_at + 8 * halves, :] = (whole - high.astype(jnp.float32)).astype(jnp.bfloat16)

    index_ref[...] = jnp.zeros_like(index_ref)
    index_ref[0:1, 0:records] = block_ref[...].astype(jnp.float32) + 1.0
    column = column_ref[...].astype(jnp.float32)
    plane = jnp.floor((column + 0.5) * (1.0 / size_y))
    index_ref[1:2, 0:records] = plane + (lax.axis_index("gx") * size_x).astype(jnp.float32)
    index_ref[2:3, 0:records] = column - plane * size_y

    total = lax.fori_loop(
        1, size_x, lambda i, acc: acc + residual_ref[i], residual_ref[0], unroll=4
    )
    total = jnp.broadcast_to(jnp.sum(total, axis=0, keepdims=True), (8, LANES))
    device = device_number(sizes)
    sums = place_sums(total, device, slabs)[0:1]
    high = sums.astype(jnp.bfloat16).astype(jnp.float32)
    middle = (sums - high).astype(jnp.bfloat16).astype(jnp.float32)
    low = sums - high - middle
    half = device // (LANES // slabs)
    row = row_of(meta_rows)
    meta = jnp.where(row == 0, index_ref[0:1, :], 0.0)
    meta = jnp.where(row == 1, index_ref[1:2, :], meta)
    meta = jnp.where(row == 2, index_ref[2:3, :], meta)
    meta = jnp.where(row == 3 + half, high, meta)
    meta = jnp.where(row == 3 + halves + half, middle, meta)
    meta = jnp.where(row == 3 + 2 * halves + half, low, meta)
    out_ref[meta_at : meta_at + meta_rows, :] = meta.astype(jnp.bfloat16)


def beside(i, above_ref, below_ref):
    return above_ref.at[min(i, DEEP - 1)] if i < REACH else below_ref.at[max(i - 2 * REACH + DEEP, 0)]


def margin_y_kernel(residual_ref, above_ref, below_ref, within_ref, across_ref):
    size_x, size_y, _ = residual_ref.shape
    row = row_of(8)

    def plane(x, at):
        if x < size_x:
            return residual_ref[x, pl.ds(at, 8), :]
        x -= size_x
        return beside(x, above_ref, below_ref)[pl.ds(at, 8), :]

    for pair in range((size_x + 2 * REACH) // 2):
        low = [plane(2 * pair + k, 0) for k in range(2)]
        high = [plane(2 * pair + k, size_y - 8) for k in range(2)]
        down = jnp.where(row < 4, low[0], pltpu.roll(low[1], 4, 0))
        up = jnp.where(row < 4, pltpu.roll(high[1], 4, 0), high[0])
        within_ref[pair], across_ref[pair] = by_parity("gy", up, down)


def edge_group(values):
    rows = values[0].shape[0]
    place, sub_of = lane_of(rows) % 16, lane_of(rows) // 16
    edge = jnp.zeros((rows, LANES), jnp.float32)
    for sub, value in enumerate(values):
        first = pltpu.roll(value, (sub * 16 + 4) % LANES, 1)
        last = pltpu.roll(value, (sub * 16 + 12) % LANES, 1)
        edge = jnp.where((sub_of == sub) & (place >= 4) & (place < 8), first, edge)
        edge = jnp.where((sub_of == sub) & (place >= 8) & (place < 12), last, edge)
    return edge


def edge_own_kernel(residual_ref, above_ref, below_ref, edge_ref):
    groups = edge_ref.shape[0]

    def group(g, carry):
        edge_ref[g] = edge_group([residual_ref[g * SUBS + sub] for sub in range(SUBS)])
        return carry

    lax.fori_loop(0, groups - 1, group, 0)
    edge_ref[groups - 1] = edge_group([beside(i, above_ref, below_ref)[...] for i in range(2 * REACH)])


def edge_tail_kernel(part_ref, within_ref, across_ref, tail_ref, edge_ref, down_ref, up_ref):
    groups, size_y, _ = part_ref.shape
    row = row_of(8)
    place = lane_of(size_y + 2 * REACH) % 16
    down = up = jnp.zeros(down_ref.shape, jnp.float32)
    for g in range(groups):
        tails = []
        for x in range(g * SUBS, g * SUBS + SUBS):
            after, before = by_parity("gy", within_ref[x // 2], across_ref[x // 2])
            if x % 2:
                after, before = pltpu.roll(after, 4, 0), pltpu.roll(before, 4, 0)
            tails.append(jnp.where(row < 4, after, before))
            tail_ref[x] = tails[-1]
        edge_ref[g, 0:size_y, :] = part_ref[g]
        edge_ref[g, size_y:, :] = edge_group(tails)
        here = (place >= DEEP * g) & (place < DEEP * (g + 1))
        down = jnp.where(here, pltpu.roll(edge_ref[g], (DEEP * g - 4) % LANES, 1), down)
        up = jnp.where(here, pltpu.roll(edge_ref[g], (DEEP * g + DEEP - 12) % LANES, 1), up)
    down_ref[...], up_ref[...] = down, up


def coarse_solve(message_refs, high_at, low_at, halves, sums):
    def body(message_ref, i, total):
        high = message_ref[i, high_at : high_at + 8 * halves, :].astype(jnp.float32)
        low = message_ref[i, low_at : low_at + 8 * halves, :].astype(jnp.float32)
        rows = high + low
        tiles = [rows[8 * h : 8 * h + 8] for h in range(halves)]
        inner = sum(tiles[h] * sums[h] for h in range(halves))
        inner = jnp.sum(inner, axis=1, keepdims=True)
        return tuple(total[h] + inner * tiles[h] for h in range(halves))

    zero = jnp.zeros((8, LANES), jnp.float32)
    total = (zero,) * halves
    for ref in message_refs:
        total = lax.fori_loop(0, ref.shape[0], functools.partial(body, ref), total, unroll=8)
    return [jnp.broadcast_to(jnp.sum(t, axis=0, keepdims=True), (8, LANES)) for t in total]


def pick(values, device, slab, slabs):
    per_half = LANES // slabs
    half = device // per_half
    chosen = values[0]
    for h in range(1, len(values)):
        chosen = jnp.where(half == h, values[h], chosen)
    index = lax.rem(device, per_half) * slabs + slab
    return jnp.take_along_axis(chosen, index, axis=1)


def y_after(value):
    return pltpu.roll(value, value.shape[0] - 1, 0)


def y_before(value):
    return pltpu.roll(value, 1, 0)


def z_after(value, edges):
    return jnp.where(lane_of(value.shape[0]) == LANES - 1, edges, pltpu.roll(value, LANES - 1, 1))


def z_before(value, edges):
    return jnp.where(lane_of(value.shape[0]) == 0, edges, pltpu.roll(value, 1, 1))


def smooth(refs, x, after, edges, before):
    u_ref, x_ref, y_ref, z_ref, h_ref = refs
    value, along_x, along_y, along_z = u_ref[x], x_ref[x], y_ref[x], z_ref[x]
    total = before + along_x * u_ref[after]
    total = total + along_y * y_after(value) + y_before(along_y * value)
    total = total + along_z * z_after(value, edges) + z_before(along_z * value, edges)
    return near * value + far * (h_ref[x] * total), along_x * value


def smooth_again(u_ref, x_ref, y_ref, z_ref, h_ref, joined_ref, applied_ref):
    size_x, size_y, _ = applied_ref.shape
    outer = size_x + 2 * REACH - 1

    def group(g, before):
        for sub in range(SUBS):
            x = g * SUBS + sub
            edges = pltpu.roll(joined_ref[g], 115 - 16 * sub, 1)
            value, before = smooth((u_ref, x_ref, y_ref, z_ref, h_ref), x, x + 1, edges, before)
            applied_ref[x] = value[0:size_y]
        return before

    lax.fori_loop(0, size_x // SUBS, group, x_ref[outer] * u_ref[outer])


def main_kernel(
    sizes, records, halves, slabs, size_x, size_y,
    message_ref, other_ref, residual_ref, above_ref, below_ref, tail_ref, edge_ref, lower_ref, upper_ref,
    direction_ref, applied_ref, stat_ref,
    key_ref, code_ref, turned_ref, left_ref, right_ref, added_ref,
    density_ref, x_ref, y_ref, z_ref, h_ref, u_ref, d_ref, inside_ref, coarse_ref,
    first_ref, second_ref, third_ref, fourth_ref,
):
    n_gx, n_gy, n_gz = sizes
    gx, gy, gz = (lax.axis_index(a) for a in AXES)
    half = message_ref.shape[0]
    wide_x, wide_y = size_x + 2 * REACH, size_y + 2 * REACH
    groups = wide_x // SUBS
    high_at, low_at, meta_at, meta_rows = message_rows(records, halves)
    f32, bf16 = jnp.float32, jnp.bfloat16
    lane = lane_of(wide_y)
    row = row_of(wide_y)
    place = lane % 16

    def roll(value, shift, axis):
        return pltpu.roll(value, shift, axis)

    def read_meta(i, total):
        for j, ref in enumerate((message_ref, other_ref)):
            tile = ref[i, meta_at : meta_at + meta_rows, :].astype(f32)
            for k in range(3):
                key_ref[k, pl.ds(i + j * half, 1), :] = tile[k : k + 1]
            total = total + tile
        return total

    total = lax.fori_loop(0, half, read_meta, jnp.zeros((meta_rows, LANES), f32), unroll=4)
    sums = [
        total[3 + h : 4 + h] + total[3 + halves + h : 4 + halves + h] + total[3 + 2 * halves + h : 4 + 2 * halves + h]
        for h in range(halves)
    ]
    coarse = coarse_solve((message_ref, other_ref), high_at, low_at, halves, sums)

    def there(ix, iy, iz):
        ok = (ix >= 0) & (ix < n_gx) & (iy >= 0) & (iy < n_gy) & (iz >= 0) & (iz < n_gz)
        return ok.astype(f32), jnp.where(ok, (ix * n_gy + iy) * n_gz + iz, 0)

    lane8 = lane_of(8)
    row8 = row_of(8)
    place8 = lane8 % 16
    constant = lambda k: jnp.full((8, LANES), k, jnp.int32)

    def main_values(ix, iy):
        ok, device = there(ix, iy, gz)
        return jnp.full((8, LANES), ok, f32), ok * pick(coarse, device, lane8 // (LANES // slabs), slabs)

    def edge_values(ix, iy):
        parts = []
        for iz, slab in ((gz - 1, slabs - 1), (gz, 0), (gz, slabs - 1), (gz + 1, 0)):
            ok, device = there(ix, iy, iz)
            parts.append((jnp.full((8, LANES), ok, f32), ok * pick(coarse, device, constant(slab), slabs)))
        out = []
        for k in range(2):
            value = jnp.where(place8 < 4, parts[0][k], parts[1][k])
            value = jnp.where(place8 >= 8, parts[2][k], value)
            out.append(jnp.where(place8 >= 12, parts[3][k], value))
        return out

    def fill(kind, values_at):
        own, after, before = values_at(gy), values_at(gy + 1), values_at(gy - 1)
        for k, ref in enumerate((inside_ref, coarse_ref)):
            ref[kind, 0:size_y, :] = jnp.concatenate([own[k]] * (size_y // 8), axis=0)
            ref[kind, size_y:wide_y, :] = jnp.where(row8 < 4, after[k], before[k])

    def beside_x(iy):
        above, below = edge_values(gx + 1, iy), edge_values(gx - 1, iy)
        return [jnp.where(lane8 < 4 * 16, a, b) for a, b in zip(above, below)]

    fill(0, lambda iy: main_values(gx, iy))
    fill(1, lambda iy: main_values(gx + 1, iy))
    fill(2, lambda iy: main_values(gx - 1, iy))
    fill(3, lambda iy: edge_values(gx, iy))
    fill(4, beside_x)

    block, plane, line = (key_ref[k, 0:half, :] + roll(key_ref[k, half : 2 * half, :], SLOT, 1) for k in range(3))
    valid = block > 0.5
    block = block - 1.0
    block_y = jnp.floor((block + 0.5) * (1.0 / n_gz))
    side = block - block_y * n_gz - gz.astype(f32)
    at_x = plane - (gx * size_x).astype(f32)
    at_y = (block_y - gy.astype(f32)) * size_y + line
    valid = valid & (at_x >= -REACH) & (at_x < size_x + REACH) & (at_y >= -REACH) & (at_y < size_y + REACH)
    at_x = jnp.where(at_x < 0, at_x + wide_x, at_x)
    at_y = jnp.where(at_y < 0, at_y + wide_y, at_y)
    at_group = jnp.floor((at_x + 0.5) * (1.0 / SUBS))
    at_sub = at_x - at_group * SUBS
    code_ref[...] = jnp.where(valid, at_group * wide_y + at_y, -1.0)
    turned_ref[...] = jnp.full(turned_ref.shape, -1.0, f32)
    turned_ref[0, 0:half, :] = jnp.where(side == 0, at_sub, -1.0)
    turned_ref[1, 0:half, :] = jnp.where((side >= -1) & (side <= 1), at_sub + SUBS * (side + 1), -1.0)
    turned_ref[0] = turned_ref[0].T
    turned_ref[1] = turned_ref[1].T

    chunk = min(half, 16)
    rows_all = left_ref.shape[0]
    row_number = lax.broadcasted_iota(jnp.int32, (rows_all, LANES), 0).astype(f32)
    source = lax.broadcasted_iota(jnp.int32, (LANES, LANES), 0)
    target = lax.broadcasted_iota(jnp.int32, (LANES, LANES), 1)
    wanted = jnp.where(target % 8 < 4, target % 4 + (LANES - 4), target % 4)
    chooser = (source == wanted).astype(bf16)
    kind = jnp.where(target % 16 < 4, 0, jnp.where(target % 16 < 12, 1, 2))
    edge_code = (target // 16 + SUBS * kind).astype(f32)

    for c in range(half // chunk):
        def build(q, carry, c=c):
            p = q + c * chunk
            at = pl.ds(q * LANES if isinstance(q, int) else pl.multiple_of(q * LANES, LANES), LANES)
            code = code_ref[pl.ds(p, 1), :]
            left_ref[:, at] = jnp.where(row_number == code, 1.0, 0.0).astype(bf16)
            rows = jnp.concatenate([message_ref[p, 0:SLOT, :], other_ref[p, 0:SLOT, :]], axis=0)
            if isinstance(p, int):
                columns = [turned_ref[k, :, p : p + 1] for k in range(2)]
            else:
                turn = lax.rem(LANES - p, LANES)
                columns = [roll(turned_ref[k], turn, 1)[:, 0:1] for k in range(2)]
            key, edge_key = (jnp.broadcast_to(column, (LANES, LANES)) for column in columns)
            key = key.astype(bf16)
            for sub in range(SUBS):
                chosen = jnp.where(key == sub, rows, jnp.zeros_like(rows))
                right_ref[at, sub * LANES : (sub + 1) * LANES] = chosen
            edges = jnp.dot(rows, chooser, preferred_element_type=f32)
            right_ref[at, SUBS * LANES :] = jnp.where(edge_key == edge_code, edges, 0.0).astype(bf16)
            return carry

        if chunk == half:
            for q in range(chunk):
                build(q, 0)
        else:
            lax.fori_loop(0, chunk, build, 0)
        for n in range(0, SUBS + 1, 2):
            columns = slice(n * LANES, min(n + 2, SUBS + 1) * LANES)
            product = jnp.dot(left_ref[...], right_ref[:, columns], preferred_element_type=f32)
            added_ref[:, columns] = product if c == 0 else added_ref[:, columns] + product

    for g in range(groups):
        lines = slice(g * wide_y, (g + 1) * wide_y)
        for sub in range(SUBS):
            x = g * SUBS + sub
            k = 0 if x < size_x else 1 if x < size_x + REACH else 2
            density_ref[x] = inside_ref[k] + added_ref[lines, sub * LANES : (sub + 1) * LANES]
        k = 3 if g < groups - 1 else 4
        density_ref[wide_x + g] = inside_ref[k] + added_ref[lines, SUBS * LANES :]

    def joined(after, before):
        return jnp.where(place == 13, roll(before, 10, 1), after)

    def edge_x_after(value, other):
        return jnp.where(lane >= LANES - 16, roll(other, LANES - 16, 1), roll(value, LANES - 16, 1))

    def edge_x_before(value, other):
        return jnp.where(lane < 16, roll(other, 16, 1), roll(value, 16, 1))

    def sweep(reach, body, carry, joined_ref, beside=None):
        def turned(g, sub):
            return roll(joined_ref[g], 115 - 16 * sub, 1)

        for x in range(-reach, 0):
            after = wide_x + x + 1 if x < -1 else 0
            carry = body(wide_x + x, after, 2, turned(groups - 1, SUBS + x), carry)

        def group(g, carry):
            if beside:
                beside(g, jnp.where(g == 0, groups - 1, g - 1), g + 1, 3)
            for sub in range(SUBS):
                x = g * SUBS + sub
                carry = body(x, x + 1, 0, turned(g, sub), carry)
            return carry

        carry = lax.fori_loop(0, groups - 1, group, carry)
        if beside:
            beside(groups - 1, groups - 2, 0, 4)
        for x in range(reach):
            carry = body(size_x + x, size_x + x + 1, 1, turned(groups - 1, x), carry)
        return carry

    def beta(one, two):
        return 2.0 / jnp.maximum(one + two, 0.5)

    for g in range(groups):
        j = wide_x + g
        value = density_ref[j]
        x_ref[j] = beta(value, edge_x_after(value, density_ref[wide_x + (g + 1) % groups]))
        y_ref[j] = beta(value, y_after(value))
        z_ref[j] = beta(value, roll(value, LANES - 1, 1))

    for g in range(groups):
        j = wide_x + g
        before_x = edge_x_before(x_ref[j], x_ref[wide_x + (g - 1) % groups])
        diagonal = x_ref[j] + before_x + y_ref[j] + y_before(y_ref[j]) + z_ref[j] + roll(z_ref[j], 1, 1)
        h = inside_ref[3 if g < groups - 1 else 4] / diagonal
        h_ref[j] = h
        residual = edge_ref[g]
        lower = roll(lower_ref[...], (4 - DEEP - DEEP * g) % LANES, 1)
        upper = roll(upper_ref[...], 12 - DEEP * g, 1)
        residual = jnp.where((place >= 4 - DEEP) & (place < 4), lower, residual)
        residual = jnp.where((place >= 12) & (place < 12 + DEEP), upper, residual)
        u_ref[j] = residual * h * (1.0 / theta)
        first_ref[g] = joined(density_ref[j], z_ref[j])

    def edge_direct(g, before_g, after_g, k):
        j, before_j, after_j = wide_x + g, wide_x + before_g, wide_x + after_g
        value, along_x, along_y, along_z = u_ref[j], x_ref[j], y_ref[j], z_ref[j]
        product_z = along_z * value
        beside = along_x * edge_x_after(value, u_ref[after_j])
        beside = beside + edge_x_before(along_x * value, x_ref[before_j] * u_ref[before_j])
        beside = beside + along_y * y_after(value) + y_before(along_y * value)
        beside = beside + along_z * roll(value, LANES - 1, 1) + roll(product_z, 1, 1)
        d_ref[j] = near * value + far * (h_ref[j] * beside) + coarse_ref[k]
        second_ref[g] = joined(value, product_z)

    def edge_image(g, before_g, after_g, k):
        j, before_j, after_j = wide_x + g, wide_x + before_g, wide_x + after_g
        value, before = d_ref[j], d_ref[before_j]
        flux_x = x_ref[j] * (value - edge_x_after(value, d_ref[after_j]))
        flux_y = y_ref[j] * (value - y_after(value))
        flux_z = z_ref[j] * (value - roll(value, LANES - 1, 1))
        image = flux_x + edge_x_before(x_ref[j], x_ref[before_j]) * (value - edge_x_before(value, before))
        image = image + (flux_y - y_before(flux_y)) + (flux_z - roll(flux_z, 1, 1))
        image = image * h_ref[j] * (1.0 / theta)
        third_ref[g] = joined(value, flux_z)
        fourth_ref[g] = joined(image, z_ref[j] * image)

    def faces(x, after, k, edges, before):
        value = density_ref[x]
        sum_x, sum_y, sum_z = (
            jnp.maximum(value + other, 0.5)
            for other in (density_ref[after], y_after(value), z_after(value, edges))
        )
        both = sum_x * sum_y
        common = 2.0 / (both * sum_z)
        along_z = common * both
        common = common * sum_z
        along_x = common * sum_y
        along_y = common * sum_x
        diagonal = before + along_x + along_y + y_before(along_y) + along_z + z_before(along_z, edges)
        h = inside_ref[k] / diagonal
        x_ref[x], y_ref[x], z_ref[x], h_ref[x] = along_x, along_y, along_z, h
        residual = residual_ref[x] if k == 0 else beside(x - size_x, above_ref, below_ref)[...]
        u_ref[x, 0:size_y, :] = residual * h[0:size_y] * (1.0 / theta)
        u_ref[x, size_y:wide_y, :] = tail_ref[x] * h[size_y:wide_y] * (1.0 / theta)
        return along_x

    sweep(REACH, faces, jnp.ones((wide_y, LANES), f32), first_ref, edge_direct)

    def direct(x, after, k, edges, before):
        value, product = smooth((u_ref, x_ref, y_ref, z_ref, h_ref), x, after, edges, before)
        d_ref[x] = value + coarse_ref[k]
        return product

    outer = wide_x - 3
    sweep(2, direct, x_ref[outer] * u_ref[outer], second_ref, edge_image)

    def image_of(x, after, k, edges, carry):
        before, *found = carry
        value = d_ref[x]
        flux_x = x_ref[x] * (value - d_ref[after])
        flux_y = y_ref[x] * (value - y_after(value))
        flux_z = z_ref[x] * (value - z_after(value, edges))
        image = (flux_x - before) + (flux_y - y_before(flux_y)) + (flux_z - z_before(flux_z, edges))
        u_ref[x] = image * h_ref[x] * (1.0 / theta)
        if k == 0:
            value, image = value[0:size_y], image[0:size_y]
            direction_ref[x] = value
            parts = (residual_ref[x] * value, value * image, image)
            found = [
                total + sum(part[8 * i : 8 * i + 8] for i in range(size_y // 8))
                for total, part in zip(found, parts)
            ]
        return (flux_x, *found)

    outer = wide_x - 2
    zero = jnp.zeros((8, LANES), f32)
    _, *found = sweep(1, image_of, (x_ref[outer] * (d_ref[outer] - d_ref[outer + 1]), zero, zero, zero), third_ref)

    folded = [jnp.sum(f, axis=0, keepdims=True) for f in found]
    line = place_sums(jnp.broadcast_to(folded[2], (8, LANES)), 0, slabs)[0:1]
    line = jnp.where(lane8[0:1] == slabs, jnp.sum(folded[0], axis=1, keepdims=True), line)
    line = jnp.where(lane8[0:1] == slabs + 1, jnp.sum(folded[1], axis=1, keepdims=True), line)

    def spread(i, carry):
        stat_ref[i] = line
        return carry

    lax.fori_loop(0, stat_ref.shape[0], spread, 0, unroll=8)

    smooth_again(u_ref, x_ref, y_ref, z_ref, h_ref, fourth_ref, applied_ref)


def finish_kernel(
    sizes, records, halves, slabs,
    stat_ref, message_ref, other_ref, direction_ref, applied_ref, pressure_ref, preconditioned_ref,
):
    high_at, low_at, _, _ = message_rows(records, halves)
    per_half = LANES // slabs
    lane1 = lane_of(1)

    def place(i, carry):
        last, *sums = carry
        for h in range(halves):
            line = stat_ref[h * per_half + i]
            last = last + line
            sums[h] = sums[h] + pltpu.roll(jnp.where(lane1 < slabs, line, 0.0), i * slabs, 1)
        return (last, *sums)

    zero = jnp.zeros((1, LANES), jnp.float32)
    last, *sums = lax.fori_loop(0, per_half, place, (zero,) * (1 + halves), unroll=8)
    coarse = coarse_solve((message_ref, other_ref), high_at, low_at, halves, sums)
    lane8 = lane_of(8)
    own = pick(coarse, device_number(sizes), lane8 // (LANES // slabs), slabs)
    alpha = last[:, slabs : slabs + 1] / last[:, slabs + 1 : slabs + 2]
    size_x, size_y, _ = direction_ref.shape
    alpha = jnp.broadcast_to(alpha, (size_y, LANES))
    own = jnp.concatenate([own] * (size_y // 8), axis=0)

    def body(x, carry):
        direction = direction_ref[x]
        pressure_ref[x] = alpha * direction
        preconditioned_ref[x] = direction - alpha * (applied_ref[x] + own)
        return carry

    lax.fori_loop(0, size_x, body, 0, unroll=2)


def cycle(value, axis, step):
    size = lax.axis_size(axis)
    return lax.ppermute(value, axis, [(i, (i + step) % size) for i in range(size)])


def swap_within(value, axis):
    return lax.ppermute(value, axis, [(i, i ^ 1) for i in range(lax.axis_size(axis))])


def swap_across(value, axis):
    size = lax.axis_size(axis)
    to = {i: i if i in (0, size - 1) else i + 1 if i % 2 else i - 1 for i in range(size)}
    return lax.ppermute(value, axis, sorted(to.items()))


def exchange(value, axis, stride):
    size = lax.axis_size(axis)
    return lax.ppermute(value, axis, [(i, i ^ stride) for i in range(size)])


def doublings():
    steps = []
    for axis in ("gy", "gx", "gz"):
        strides = [1 << k for k in range(lax.axis_size(axis).bit_length() - 1)]
        steps += [(axis, stride) for stride in strides[::-1]]
    return steps


def shards(sizes, right_side, coarse_inverse, sphere_rows, margin_block, margin_column):
    size_x, size_y, _ = right_side.shape
    slabs, subdomains = coarse_inverse.shape
    records = sphere_rows.shape[0]
    halves = subdomains // LANES
    devices = sizes[0] * sizes[1] * sizes[2]
    wide_x, wide_y = size_x + 2 * REACH, size_y + 2 * REACH
    groups = wide_x // SUBS
    planes = wide_x + groups
    f32, bf16 = jnp.float32, jnp.bfloat16
    _, _, meta_at, meta_rows = message_rows(records, halves)
    shape = jax.ShapeDtypeStruct

    def call(kernel, out_shape, operands, scratch=(), results=pltpu.VMEM, mib=8, left=()):
        outs = [results(o.shape, o.dtype) for o in out_shape]
        return pl.pallas_call(
            kernel,
            out_shape=outs,
            in_specs=[VMEM] * len(operands),
            out_specs=[VMEM] * len(outs),
            scratch_shapes=list(scratch),
            compiler_params=pltpu.CompilerParams(vmem_limit_bytes=mib << 20),
        )(*(pltpu.with_memory_space_constraint(o, pltpu.HBM if i in left else pltpu.VMEM) for i, o in enumerate(operands)))

    planes_sent = shape((DEEP, size_y, LANES), f32)
    swap = sizes[0] == 2
    message, *margin = call(
        functools.partial(pack_kernel, sizes),
        (shape((meta_at + meta_rows, LANES), bf16),) + (planes_sent,) * (1 if swap else 2),
        (right_side, coarse_inverse, sphere_rows, margin_block.reshape(1, records), margin_column.reshape(1, records)),
        (pltpu.VMEM((8, LANES), f32),),
        left=(1, 2, 3, 4),
    )
    steps = doublings()

    def join(k, held):
        return exchange(held, *steps[k])

    held = message[None]
    received = join(0, held)
    if swap:
        above = below = cycle(margin[0], "gx", 1)
    else:
        above, below = cycle(margin[0], "gx", -1), cycle(margin[1], "gx", 1)
    held, received, above, below = lax.optimization_barrier((held, received, above, below))
    held = jnp.concatenate([held, received], axis=0)
    received = join(1, held)
    pairs = shape((wide_x // 2, 8, LANES), f32)
    within, across = call(margin_y_kernel, (pairs, pairs), (right_side, above, below))
    within = swap_within(within, "gy")
    across = swap_across(across, "gy")
    (part,) = call(edge_own_kernel, (shape((groups, size_y, LANES), f32),), (right_side, above, below))
    held = jnp.concatenate([held, received], axis=0)
    received = join(2, held)
    line = shape((wide_y, LANES), f32)
    tail, edge, down, up = call(
        edge_tail_kernel,
        (shape((wide_x, 8, LANES), f32), shape((groups, wide_y, LANES), f32), line, line),
        (part, within, across),
    )
    lower = cycle(up, "gz", 1)
    upper = cycle(down, "gz", -1)
    for k in range(3, len(steps)):
        held = jnp.concatenate([held, received], axis=0)
        received = join(k, held)

    half = devices // 2
    depth = min(half, 16) * LANES
    rows_all = 16 * pl.cdiv(groups * wide_y, 16)
    field = pltpu.VMEM((planes, wide_y, LANES), f32)
    edges = (groups, wide_y, LANES)
    margin = pltpu.VMEM(edges, f32)
    kinds = pltpu.VMEM((5, wide_y, LANES), f32)
    block = shape((size_x, size_y, LANES), f32)
    direction, applied, stats = call(
        functools.partial(main_kernel, sizes, records, halves, slabs, size_x, size_y),
        (block, block, shape((devices, 1, LANES), f32)),
        (held, received, right_side, above, below, tail, edge, lower, upper),
        (
            pltpu.VMEM((3, devices, LANES), f32),
            pltpu.VMEM((half, LANES), f32),
            pltpu.VMEM((2, LANES, LANES), f32),
            pltpu.VMEM((rows_all, depth), bf16),
            pltpu.VMEM((depth, (SUBS + 1) * LANES), bf16),
            pltpu.VMEM((rows_all, (SUBS + 1) * LANES), f32),
            field, field, field, field, field, field, field, kinds, kinds, margin, margin, margin, margin,
        ),
        mib=28,
    )
    stats = lax.all_to_all(stats, AXES, 0, 0, tiled=True)
    return call(
        functools.partial(finish_kernel, sizes, records, halves, slabs),
        (block, block),
        (stats, held, received, direction, applied),
        results=shape,
    )


def solution(mesh):
    placed = (
        P("gx", "gy", "gz"),
        P(("gx", "gy", "gz"), None),
        P(("gx", "gy", "gz"), None),
        P(("gx", "gy", "gz"), None),
        P(("gx", "gy", "gz")),
    )
    sizes = tuple(mesh.shape[axis] for axis in AXES)

    def body(*operands):
        return shards(sizes, *operands)

    return jax.shard_map(
        body,
        mesh=mesh,
        in_specs=placed,
        out_specs=(P("gx", "gy", "gz"), P("gx", "gy", "gz")),
        check_vma=False,
    )
```

```python
import functools

import jax
import jax.numpy as jnp
from jax import lax
from jax.experimental import pallas as pl
from jax.experimental.pallas import tpu as pltpu
from jax.sharding import PartitionSpec as P


bound_low = 0.1
bound_high = 2.0
theta = 0.5 * (bound_high + bound_low)
delta = 0.5 * (bound_high - bound_low)
weight_first = delta / theta
weight_second = 1.0 / (2.0 * theta / delta - weight_first)
far = 2.0 * weight_second / delta
near = 1.0 + weight_second * weight_first + far * (theta - 1.0)

AXES = ("gx", "gy", "gz")
LANES = 128
REACH = 4
DEEP = 3
SUBS = 8
SLOT = 64
EXACT = lax.Precision.HIGHEST
VMEM = pl.BlockSpec(memory_space=pltpu.VMEM)


def lane_of(rows):
    return lax.broadcasted_iota(jnp.int32, (rows, LANES), 1)


def row_of(rows):
    return lax.broadcasted_iota(jnp.int32, (rows, LANES), 0)


def by_parity(axis, one, two):
    even = lax.axis_index(axis) % 2 == 0
    return jnp.where(even, one, two), jnp.where(even, two, one)


def message_rows(records, halves):
    meta = 16 * pl.cdiv(3 + 3 * halves, 16)
    return records, records + 8 * halves, records + 16 * halves, meta


def place_sums(total, device, slabs):
    width = LANES // slabs
    base = lax.rem(device, width) * slabs
    source = lax.broadcasted_iota(jnp.int32, (LANES, LANES), 0)
    target = lax.broadcasted_iota(jnp.int32, (LANES, LANES), 1)
    first = (target - base) * width
    chosen = (source >= first) & (source < first + width) & (target >= base) & (target < base + slabs)
    return jnp.dot(total, chosen.astype(jnp.float32), precision=EXACT, preferred_element_type=jnp.float32)


def device_number(sizes):
    return (lax.axis_index("gx") * sizes[1] + lax.axis_index("gy")) * sizes[2] + lax.axis_index("gz")


def pack_kernel(sizes, residual_ref, inverse_ref, rows_ref, block_ref, column_ref, out_ref, *rest):
    *margin_refs, index_ref = rest
    size_x, size_y, _ = residual_ref.shape
    slabs, subdomains = inverse_ref.shape
    records = rows_ref.shape[0]
    halves = subdomains // LANES
    high_at, low_at, meta_at, meta_rows = message_rows(records, halves)
    out_ref[0:records, :] = rows_ref[...]
    own = (slice(0, DEEP), slice(size_x - DEEP, size_x))
    if len(margin_refs) == 1:
        is_first = lax.axis_index("gx") == 0
        margin_refs[0][...] = jnp.where(is_first, residual_ref[own[1]], residual_ref[own[0]])
    else:
        margin_refs[0][...], margin_refs[1][...] = residual_ref[own[0]], residual_ref[own[1]]
    whole = jnp.concatenate([inverse_ref[:, h * LANES : (h + 1) * LANES] for h in range(halves)], axis=0)
    high = whole.astype(jnp.bfloat16)
    out_ref[high_at : high_at + 8 * halves, :] = high
    out_ref[low_at : low_at + 8 * halves, :] = (whole - high.astype(jnp.float32)).astype(jnp.bfloat16)

    index_ref[...] = jnp.zeros_like(index_ref)
    index_ref[0:1, 0:records] = block_ref[...].astype(jnp.float32) + 1.0
    column = column_ref[...].astype(jnp.float32)
    plane = jnp.floor((column + 0.5) * (1.0 / size_y))
    index_ref[1:2, 0:records] = plane + (lax.axis_index("gx") * size_x).astype(jnp.float32)
    index_ref[2:3, 0:records] = column - plane * size_y

    total = lax.fori_loop(
        1, size_x, lambda i, acc: acc + residual_ref[i], residual_ref[0], unroll=4
    )
    total = jnp.broadcast_to(jnp.sum(total, axis=0, keepdims=True), (8, LANES))
    device = device_number(sizes)
    sums = place_sums(total, device, slabs)[0:1]
    high = sums.astype(jnp.bfloat16).astype(jnp.float32)
    middle = (sums - high).astype(jnp.bfloat16).astype(jnp.float32)
    low = sums - high - middle
    half = device // (LANES // slabs)
    row = row_of(meta_rows)
    meta = jnp.where(row == 0, index_ref[0:1, :], 0.0)
    meta = jnp.where(row == 1, index_ref[1:2, :], meta)
    meta = jnp.where(row == 2, index_ref[2:3, :], meta)
    meta = jnp.where(row == 3 + half, high, meta)
    meta = jnp.where(row == 3 + halves + half, middle, meta)
    meta = jnp.where(row == 3 + 2 * halves + half, low, meta)
    out_ref[meta_at : meta_at + meta_rows, :] = meta.astype(jnp.bfloat16)


def beside(i, above_ref, below_ref):
    return above_ref.at[min(i, DEEP - 1)] if i < REACH else below_ref.at[max(i - 2 * REACH + DEEP, 0)]


def margin_y_kernel(residual_ref, above_ref, below_ref, within_ref, across_ref):
    size_x, size_y, _ = residual_ref.shape
    row = row_of(8)

    def plane(x, at):
        if x < size_x:
            return residual_ref[x, pl.ds(at, 8), :]
        x -= size_x
        return beside(x, above_ref, below_ref)[pl.ds(at, 8), :]

    for pair in range((size_x + 2 * REACH) // 2):
        low = [plane(2 * pair + k, 0) for k in range(2)]
        high = [plane(2 * pair + k, size_y - 8) for k in range(2)]
        down = jnp.where(row < 4, low[0], pltpu.roll(low[1], 4, 0))
        up = jnp.where(row < 4, pltpu.roll(high[1], 4, 0), high[0])
        within_ref[pair], across_ref[pair] = by_parity("gy", up, down)


def edge_group(values):
    rows = values[0].shape[0]
    place, sub_of = lane_of(rows) % 16, lane_of(rows) // 16
    edge = jnp.zeros((rows, LANES), jnp.float32)
    for sub, value in enumerate(values):
        first = pltpu.roll(value, (sub * 16 + 4) % LANES, 1)
        last = pltpu.roll(value, (sub * 16 + 12) % LANES, 1)
        edge = jnp.where((sub_of == sub) & (place >= 4) & (place < 8), first, edge)
        edge = jnp.where((sub_of == sub) & (place >= 8) & (place < 12), last, edge)
    return edge


def edge_own_kernel(residual_ref, above_ref, below_ref, edge_ref):
    groups = edge_ref.shape[0]

    def group(g, carry):
        edge_ref[g] = edge_group([residual_ref[g * SUBS + sub] for sub in range(SUBS)])
        return carry

    lax.fori_loop(0, groups - 1, group, 0)
    edge_ref[groups - 1] = edge_group([beside(i, above_ref, below_ref)[...] for i in range(2 * REACH)])


def edge_tail_kernel(part_ref, within_ref, across_ref, tail_ref, edge_ref, down_ref, up_ref):
    groups, size_y, _ = part_ref.shape
    row = row_of(8)
    place = lane_of(size_y + 2 * REACH) % 16
    down = up = jnp.zeros(down_ref.shape, jnp.float32)
    for g in range(groups):
        tails = []
        for x in range(g * SUBS, g * SUBS + SUBS):
            after, before = by_parity("gy", within_ref[x // 2], across_ref[x // 2])
            if x % 2:
                after, before = pltpu.roll(after, 4, 0), pltpu.roll(before, 4, 0)
            tails.append(jnp.where(row < 4, after, before))
            tail_ref[x] = tails[-1]
        edge_ref[g, 0:size_y, :] = part_ref[g]
        edge_ref[g, size_y:, :] = edge_group(tails)
        here = (place >= DEEP * g) & (place < DEEP * (g + 1))
        down = jnp.where(here, pltpu.roll(edge_ref[g], (DEEP * g - 4) % LANES, 1), down)
        up = jnp.where(here, pltpu.roll(edge_ref[g], (DEEP * g + DEEP - 12) % LANES, 1), up)
    down_ref[...], up_ref[...] = down, up


def coarse_solve(message_refs, high_at, low_at, halves, sums):
    def body(message_ref, i, total):
        high = message_ref[i, high_at : high_at + 8 * halves, :].astype(jnp.float32)
        low = message_ref[i, low_at : low_at + 8 * halves, :].astype(jnp.float32)
        rows = high + low
        tiles = [rows[8 * h : 8 * h + 8] for h in range(halves)]
        inner = sum(tiles[h] * sums[h] for h in range(halves))
        inner = jnp.sum(inner, axis=1, keepdims=True)
        return tuple(total[h] + inner * tiles[h] for h in range(halves))

    zero = jnp.zeros((8, LANES), jnp.float32)
    total = (zero,) * halves
    for ref in message_refs:
        total = lax.fori_loop(0, ref.shape[0], functools.partial(body, ref), total, unroll=16)
    return [jnp.broadcast_to(jnp.sum(t, axis=0, keepdims=True), (8, LANES)) for t in total]


def pick(values, device, slab, slabs):
    per_half = LANES // slabs
    half = device // per_half
    chosen = values[0]
    for h in range(1, len(values)):
        chosen = jnp.where(half == h, values[h], chosen)
    index = lax.rem(device, per_half) * slabs + slab
    return jnp.take_along_axis(chosen, index, axis=1)


def y_after(value):
    return pltpu.roll(value, value.shape[0] - 1, 0)


def y_before(value):
    return pltpu.roll(value, 1, 0)


def z_after(value, edges):
    return jnp.where(lane_of(value.shape[0]) == LANES - 1, edges, pltpu.roll(value, LANES - 1, 1))


def z_before(value, edges):
    return jnp.where(lane_of(value.shape[0]) == 0, edges, pltpu.roll(value, 1, 1))


def smooth(refs, x, after, edges, before):
    u_ref, x_ref, y_ref, z_ref, h_ref = refs
    value, along_x, along_y, along_z = u_ref[x], x_ref[x], y_ref[x], z_ref[x]
    total = before + along_x * u_ref[after]
    total = total + along_y * y_after(value) + y_before(along_y * value)
    total = total + along_z * z_after(value, edges) + z_before(along_z * value, edges)
    return near * value + far * (h_ref[x] * total), along_x * value


def smooth_again(u_ref, x_ref, y_ref, z_ref, h_ref, joined_ref, applied_ref):
    size_x, size_y, _ = applied_ref.shape
    outer = size_x + 2 * REACH - 1

    def group(g, before):
        for sub in range(SUBS):
            x = g * SUBS + sub
            edges = pltpu.roll(joined_ref[g], 115 - 16 * sub, 1)
            value, before = smooth((u_ref, x_ref, y_ref, z_ref, h_ref), x, x + 1, edges, before)
            applied_ref[x] = value[0:size_y]
        return before

    lax.fori_loop(0, size_x // SUBS, group, x_ref[outer] * u_ref[outer])


def main_kernel(
    sizes, records, halves, slabs, size_x, size_y,
    message_ref, other_ref, residual_ref, above_ref, below_ref, tail_ref, edge_ref, lower_ref, upper_ref,
    direction_ref, applied_ref, stat_ref,
    key_ref, code_ref, turned_ref, left_ref, right_ref, added_ref,
    density_ref, x_ref, y_ref, z_ref, h_ref, u_ref, d_ref, inside_ref, coarse_ref,
    first_ref, second_ref, third_ref, fourth_ref,
):
    n_gx, n_gy, n_gz = sizes
    gx, gy, gz = (lax.axis_index(a) for a in AXES)
    half = message_ref.shape[0]
    wide_x, wide_y = size_x + 2 * REACH, size_y + 2 * REACH
    groups = wide_x // SUBS
    high_at, low_at, meta_at, meta_rows = message_rows(records, halves)
    f32, bf16 = jnp.float32, jnp.bfloat16
    lane = lane_of(wide_y)
    row = row_of(wide_y)
    place = lane % 16

    def roll(value, shift, axis):
        return pltpu.roll(value, shift, axis)

    def read_meta(i, total):
        for j, ref in enumerate((message_ref, other_ref)):
            tile = ref[i, meta_at : meta_at + meta_rows, :].astype(f32)
            for k in range(3):
                key_ref[k, pl.ds(i + j * half, 1), :] = tile[k : k + 1]
            total = total + tile
        return total

    total = lax.fori_loop(0, half, read_meta, jnp.zeros((meta_rows, LANES), f32), unroll=16)
    sums = [
        total[3 + h : 4 + h] + total[3 + halves + h : 4 + halves + h] + total[3 + 2 * halves + h : 4 + 2 * halves + h]
        for h in range(halves)
    ]
    coarse = coarse_solve((message_ref, other_ref), high_at, low_at, halves, sums)

    def there(ix, iy, iz):
        ok = (ix >= 0) & (ix < n_gx) & (iy >= 0) & (iy < n_gy) & (iz >= 0) & (iz < n_gz)
        return ok.astype(f32), jnp.where(ok, (ix * n_gy + iy) * n_gz + iz, 0)

    lane8 = lane_of(8)
    row8 = row_of(8)
    place8 = lane8 % 16
    constant = lambda k: jnp.full((8, LANES), k, jnp.int32)

    def main_values(ix, iy):
        ok, device = there(ix, iy, gz)
        return jnp.full((8, LANES), ok, f32), ok * pick(coarse, device, lane8 // (LANES // slabs), slabs)

    def edge_values(ix, iy):
        parts = []
        for iz, slab in ((gz - 1, slabs - 1), (gz, 0), (gz, slabs - 1), (gz + 1, 0)):
            ok, device = there(ix, iy, iz)
            parts.append((jnp.full((8, LANES), ok, f32), ok * pick(coarse, device, constant(slab), slabs)))
        out = []
        for k in range(2):
            value = jnp.where(place8 < 4, parts[0][k], parts[1][k])
            value = jnp.where(place8 >= 8, parts[2][k], value)
            out.append(jnp.where(place8 >= 12, parts[3][k], value))
        return out

    def fill(kind, values_at):
        own, after, before = values_at(gy), values_at(gy + 1), values_at(gy - 1)
        for k, ref in enumerate((inside_ref, coarse_ref)):
            ref[kind, 0:size_y, :] = jnp.concatenate([own[k]] * (size_y // 8), axis=0)
            ref[kind, size_y:wide_y, :] = jnp.where(row8 < 4, after[k], before[k])

    def beside_x(iy):
        above, below = edge_values(gx + 1, iy), edge_values(gx - 1, iy)
        return [jnp.where(lane8 < 4 * 16, a, b) for a, b in zip(above, below)]

    fill(0, lambda iy: main_values(gx, iy))
    fill(1, lambda iy: main_values(gx + 1, iy))
    fill(2, lambda iy: main_values(gx - 1, iy))
    fill(3, lambda iy: edge_values(gx, iy))
    fill(4, beside_x)

    block, plane, line = (key_ref[k, 0:half, :] + roll(key_ref[k, half : 2 * half, :], SLOT, 1) for k in range(3))
    valid = block > 0.5
    block = block - 1.0
    block_y = jnp.floor((block + 0.5) * (1.0 / n_gz))
    side = block - block_y * n_gz - gz.astype(f32)
    at_x = plane - (gx * size_x).astype(f32)
    at_y = (block_y - gy.astype(f32)) * size_y + line
    valid = valid & (at_x >= -REACH) & (at_x < size_x + REACH) & (at_y >= -REACH) & (at_y < size_y + REACH)
    at_x = jnp.where(at_x < 0, at_x + wide_x, at_x)
    at_y = jnp.where(at_y < 0, at_y + wide_y, at_y)
    at_group = jnp.floor((at_x + 0.5) * (1.0 / SUBS))
    at_sub = at_x - at_group * SUBS
    code_ref[...] = jnp.where(valid, at_group * wide_y + at_y, -1.0)
    turned_ref[...] = jnp.full(turned_ref.shape, -1.0, f32)
    turned_ref[0, 0:half, :] = jnp.where(side == 0, at_sub, -1.0)
    turned_ref[1, 0:half, :] = jnp.where((side >= -1) & (side <= 1), at_sub + SUBS * (side + 1), -1.0)
    turned_ref[0] = turned_ref[0].T
    turned_ref[1] = turned_ref[1].T

    chunk = min(half, 16)
    rows_all = left_ref.shape[0]
    row_number = lax.broadcasted_iota(jnp.int32, (rows_all, LANES), 0).astype(f32)
    source = lax.broadcasted_iota(jnp.int32, (LANES, LANES), 0)
    target = lax.broadcasted_iota(jnp.int32, (LANES, LANES), 1)
    wanted = jnp.where(target % 8 < 4, target % 4 + (LANES - 4), target % 4)
    chooser = (source == wanted).astype(bf16)
    kind = jnp.where(target % 16 < 4, 0, jnp.where(target % 16 < 12, 1, 2))
    edge_code = (target // 16 + SUBS * kind).astype(f32)

    for c in range(half // chunk):
        def build(q, carry, c=c):
            p = q + c * chunk
            at = pl.ds(q * LANES if isinstance(q, int) else pl.multiple_of(q * LANES, LANES), LANES)
            code = code_ref[pl.ds(p, 1), :]
            left_ref[:, at] = jnp.where(row_number == code, 1.0, 0.0).astype(bf16)
            rows = jnp.concatenate([message_ref[p, 0:SLOT, :], other_ref[p, 0:SLOT, :]], axis=0)
            if isinstance(p, int):
                columns = [turned_ref[k, :, p : p + 1] for k in range(2)]
            else:
                turn = lax.rem(LANES - p, LANES)
                columns = [roll(turned_ref[k], turn, 1)[:, 0:1] for k in range(2)]
            key, edge_key = (jnp.broadcast_to(column, (LANES, LANES)) for column in columns)
            key = key.astype(bf16)
            for sub in range(SUBS):
                chosen = jnp.where(key == sub, rows, jnp.zeros_like(rows))
                right_ref[at, sub * LANES : (sub + 1) * LANES] = chosen
            edges = jnp.dot(rows, chooser, preferred_element_type=f32)
            right_ref[at, SUBS * LANES :] = jnp.where(edge_key == edge_code, edges, 0.0).astype(bf16)
            return carry

        if chunk == half:
            for q in range(chunk):
                build(q, 0)
        else:
            lax.fori_loop(0, chunk, build, 0)
        for n in range(0, SUBS + 1, 2):
            columns = slice(n * LANES, min(n + 2, SUBS + 1) * LANES)
            product = jnp.dot(left_ref[...], right_ref[:, columns], preferred_element_type=f32)
            added_ref[:, columns] = product if c == 0 else added_ref[:, columns] + product

    for g in range(groups):
        lines = slice(g * wide_y, (g + 1) * wide_y)
        for sub in range(SUBS):
            x = g * SUBS + sub
            k = 0 if x < size_x else 1 if x < size_x + REACH else 2
            density_ref[x] = inside_ref[k] + added_ref[lines, sub * LANES : (sub + 1) * LANES]
        k = 3 if g < groups - 1 else 4
        density_ref[wide_x + g] = inside_ref[k] + added_ref[lines, SUBS * LANES :]

    def joined(after, before):
        return jnp.where(place == 13, roll(before, 10, 1), after)

    def edge_x_after(value, other):
        return jnp.where(lane >= LANES - 16, roll(other, LANES - 16, 1), roll(value, LANES - 16, 1))

    def edge_x_before(value, other):
        return jnp.where(lane < 16, roll(other, 16, 1), roll(value, 16, 1))

    def sweep(reach, body, carry, joined_ref, beside=None):
        def turned(g, sub):
            return roll(joined_ref[g], 115 - 16 * sub, 1)

        for x in range(-reach, 0):
            after = wide_x + x + 1 if x < -1 else 0
            carry = body(wide_x + x, after, 2, turned(groups - 1, SUBS + x), carry)

        def group(g, carry):
            if beside:
                beside(g, jnp.where(g == 0, groups - 1, g - 1), g + 1, 3)
            for sub in range(SUBS):
                x = g * SUBS + sub
                carry = body(x, x + 1, 0, turned(g, sub), carry)
            return carry

        carry = lax.fori_loop(0, groups - 1, group, carry)
        if beside:
            beside(groups - 1, groups - 2, 0, 4)
        for x in range(reach):
            carry = body(size_x + x, size_x + x + 1, 1, turned(groups - 1, x), carry)
        return carry

    def beta(one, two):
        return 2.0 / jnp.maximum(one + two, 0.5)

    for g in range(groups):
        j = wide_x + g
        value = density_ref[j]
        x_ref[j] = beta(value, edge_x_after(value, density_ref[wide_x + (g + 1) % groups]))
        y_ref[j] = beta(value, y_after(value))
        z_ref[j] = beta(value, roll(value, LANES - 1, 1))

    for g in range(groups):
        j = wide_x + g
        before_x = edge_x_before(x_ref[j], x_ref[wide_x + (g - 1) % groups])
        diagonal = x_ref[j] + before_x + y_ref[j] + y_before(y_ref[j]) + z_ref[j] + roll(z_ref[j], 1, 1)
        h = inside_ref[3 if g < groups - 1 else 4] / diagonal
        h_ref[j] = h
        residual = edge_ref[g]
        lower = roll(lower_ref[...], (4 - DEEP - DEEP * g) % LANES, 1)
        upper = roll(upper_ref[...], 12 - DEEP * g, 1)
        residual = jnp.where((place >= 4 - DEEP) & (place < 4), lower, residual)
        residual = jnp.where((place >= 12) & (place < 12 + DEEP), upper, residual)
        u_ref[j] = residual * h * (1.0 / theta)
        first_ref[g] = joined(density_ref[j], z_ref[j])

    def edge_direct(g, before_g, after_g, k):
        j, before_j, after_j = wide_x + g, wide_x + before_g, wide_x + after_g
        value, along_x, along_y, along_z = u_ref[j], x_ref[j], y_ref[j], z_ref[j]
        product_z = along_z * value
        beside = along_x * edge_x_after(value, u_ref[after_j])
        beside = beside + edge_x_before(along_x * value, x_ref[before_j] * u_ref[before_j])
        beside = beside + along_y * y_after(value) + y_before(along_y * value)
        beside = beside + along_z * roll(value, LANES - 1, 1) + roll(product_z, 1, 1)
        d_ref[j] = near * value + far * (h_ref[j] * beside) + coarse_ref[k]
        second_ref[g] = joined(value, product_z)

    def edge_image(g, before_g, after_g, k):
        j, before_j, after_j = wide_x + g, wide_x + before_g, wide_x + after_g
        value, before = d_ref[j], d_ref[before_j]
        flux_x = x_ref[j] * (value - edge_x_after(value, d_ref[after_j]))
        flux_y = y_ref[j] * (value - y_after(value))
        flux_z = z_ref[j] * (value - roll(value, LANES - 1, 1))
        image = flux_x + edge_x_before(x_ref[j], x_ref[before_j]) * (value - edge_x_before(value, before))
        image = image + (flux_y - y_before(flux_y)) + (flux_z - roll(flux_z, 1, 1))
        image = image * h_ref[j] * (1.0 / theta)
        third_ref[g] = joined(value, flux_z)
        fourth_ref[g] = joined(image, z_ref[j] * image)

    def faces(x, after, k, edges, before):
        value = density_ref[x]
        sum_x, sum_y, sum_z = (
            jnp.maximum(value + other, 0.5)
            for other in (density_ref[after], y_after(value), z_after(value, edges))
        )
        both = sum_x * sum_y
        common = 2.0 / (both * sum_z)
        along_z = common * both
        common = common * sum_z
        along_x = common * sum_y
        along_y = common * sum_x
        diagonal = before + along_x + along_y + y_before(along_y) + along_z + z_before(along_z, edges)
        h = inside_ref[k] / diagonal
        x_ref[x], y_ref[x], z_ref[x], h_ref[x] = along_x, along_y, along_z, h
        residual = residual_ref[x] if k == 0 else beside(x - size_x, above_ref, below_ref)[...]
        u_ref[x, 0:size_y, :] = residual * h[0:size_y] * (1.0 / theta)
        u_ref[x, size_y:wide_y, :] = tail_ref[x] * h[size_y:wide_y] * (1.0 / theta)
        return along_x

    sweep(REACH, faces, jnp.ones((wide_y, LANES), f32), first_ref, edge_direct)

    def direct(x, after, k, edges, before):
        value, product = smooth((u_ref, x_ref, y_ref, z_ref, h_ref), x, after, edges, before)
        d_ref[x] = value + coarse_ref[k]
        return product

    outer = wide_x - 3
    sweep(2, direct, x_ref[outer] * u_ref[outer], second_ref, edge_image)

    def image_of(x, after, k, edges, carry):
        before, *found = carry
        value = d_ref[x]
        flux_x = x_ref[x] * (value - d_ref[after])
        flux_y = y_ref[x] * (value - y_after(value))
        flux_z = z_ref[x] * (value - z_after(value, edges))
        image = (flux_x - before) + (flux_y - y_before(flux_y)) + (flux_z - z_before(flux_z, edges))
        u_ref[x] = image * h_ref[x] * (1.0 / theta)
        if k == 0:
            value, image = value[0:size_y], image[0:size_y]
            direction_ref[x] = value
            parts = (residual_ref[x] * value, value * image, image)
            found = [
                total + sum(part[8 * i : 8 * i + 8] for i in range(size_y // 8))
                for total, part in zip(found, parts)
            ]
        return (flux_x, *found)

    outer = wide_x - 2
    zero = jnp.zeros((8, LANES), f32)
    _, *found = sweep(1, image_of, (x_ref[outer] * (d_ref[outer] - d_ref[outer + 1]), zero, zero, zero), third_ref)

    folded = [jnp.sum(f, axis=0, keepdims=True) for f in found]
    line = place_sums(jnp.broadcast_to(folded[2], (8, LANES)), 0, slabs)[0:1]
    line = jnp.where(lane8[0:1] == slabs, jnp.sum(folded[0], axis=1, keepdims=True), line)
    line = jnp.where(lane8[0:1] == slabs + 1, jnp.sum(folded[1], axis=1, keepdims=True), line)

    def spread(i, carry):
        stat_ref[i] = line
        return carry

    lax.fori_loop(0, stat_ref.shape[0], spread, 0, unroll=8)

    smooth_again(u_ref, x_ref, y_ref, z_ref, h_ref, fourth_ref, applied_ref)


def finish_kernel(
    sizes, records, halves, slabs,
    stat_ref, message_ref, other_ref, direction_ref, applied_ref, pressure_ref, preconditioned_ref,
):
    high_at, low_at, _, _ = message_rows(records, halves)
    per_half = LANES // slabs
    lane1 = lane_of(1)

    def place(i, carry):
        last, *sums = carry
        for h in range(halves):
            line = stat_ref[h * per_half + i]
            last = last + line
            sums[h] = sums[h] + pltpu.roll(jnp.where(lane1 < slabs, line, 0.0), i * slabs, 1)
        return (last, *sums)

    zero = jnp.zeros((1, LANES), jnp.float32)
    last, *sums = lax.fori_loop(0, per_half, place, (zero,) * (1 + halves), unroll=8)
    coarse = coarse_solve((message_ref, other_ref), high_at, low_at, halves, sums)
    lane8 = lane_of(8)
    own = pick(coarse, device_number(sizes), lane8 // (LANES // slabs), slabs)
    alpha = last[:, slabs : slabs + 1] / last[:, slabs + 1 : slabs + 2]
    size_x, size_y, _ = direction_ref.shape
    alpha = jnp.broadcast_to(alpha, (size_y, LANES))
    own = jnp.concatenate([own] * (size_y // 8), axis=0)

    def body(x, carry):
        direction = direction_ref[x]
        pressure_ref[x] = alpha * direction
        preconditioned_ref[x] = direction - alpha * (applied_ref[x] + own)
        return carry

    lax.fori_loop(0, size_x, body, 0, unroll=8)


def cycle(value, axis, step):
    size = lax.axis_size(axis)
    return lax.ppermute(value, axis, [(i, (i + step) % size) for i in range(size)])


def swap_within(value, axis):
    return lax.ppermute(value, axis, [(i, i ^ 1) for i in range(lax.axis_size(axis))])


def swap_across(value, axis):
    size = lax.axis_size(axis)
    to = {i: i if i in (0, size - 1) else i + 1 if i % 2 else i - 1 for i in range(size)}
    return lax.ppermute(value, axis, sorted(to.items()))


def exchange(value, axis, stride):
    size = lax.axis_size(axis)
    return lax.ppermute(value, axis, [(i, i ^ stride) for i in range(size)])


def doublings():
    steps = []
    for axis in ("gy", "gx", "gz"):
        strides = [1 << k for k in range(lax.axis_size(axis).bit_length() - 1)]
        steps += [(axis, stride) for stride in strides[::-1]]
    return steps


def shards(sizes, right_side, coarse_inverse, sphere_rows, margin_block, margin_column):
    size_x, size_y, _ = right_side.shape
    slabs, subdomains = coarse_inverse.shape
    records = sphere_rows.shape[0]
    halves = subdomains // LANES
    devices = sizes[0] * sizes[1] * sizes[2]
    wide_x, wide_y = size_x + 2 * REACH, size_y + 2 * REACH
    groups = wide_x // SUBS
    planes = wide_x + groups
    f32, bf16 = jnp.float32, jnp.bfloat16
    _, _, meta_at, meta_rows = message_rows(records, halves)
    shape = jax.ShapeDtypeStruct

    def call(kernel, out_shape, operands, scratch=(), results=pltpu.VMEM, mib=8, left=()):
        outs = [results(o.shape, o.dtype) for o in out_shape]
        return pl.pallas_call(
            kernel,
            out_shape=outs,
            in_specs=[VMEM] * len(operands),
            out_specs=[VMEM] * len(outs),
            scratch_shapes=list(scratch),
            compiler_params=pltpu.CompilerParams(vmem_limit_bytes=mib << 20),
        )(*(pltpu.with_memory_space_constraint(o, pltpu.HBM if i in left else pltpu.VMEM) for i, o in enumerate(operands)))

    planes_sent = shape((DEEP, size_y, LANES), f32)
    swap = sizes[0] == 2
    message, *margin = call(
        functools.partial(pack_kernel, sizes),
        (shape((meta_at + meta_rows, LANES), bf16),) + (planes_sent,) * (1 if swap else 2),
        (right_side, coarse_inverse, sphere_rows, margin_block.reshape(1, records), margin_column.reshape(1, records)),
        (pltpu.VMEM((8, LANES), f32),),
        left=(1, 2, 3, 4),
    )
    steps = doublings()

    def join(k, held):
        return exchange(held, *steps[k])

    held = message[None]
    received = join(0, held)
    if swap:
        above = below = cycle(margin[0], "gx", 1)
    else:
        above, below = cycle(margin[0], "gx", -1), cycle(margin[1], "gx", 1)
    held, received, above, below = lax.optimization_barrier((held, received, above, below))
    held = jnp.concatenate([held, received], axis=0)
    received = join(1, held)
    pairs = shape((wide_x // 2, 8, LANES), f32)
    within, across = call(margin_y_kernel, (pairs, pairs), (right_side, above, below))
    within = swap_within(within, "gy")
    across = swap_across(across, "gy")
    (part,) = call(edge_own_kernel, (shape((groups, size_y, LANES), f32),), (right_side, above, below))
    held = jnp.concatenate([held, received], axis=0)
    received = join(2, held)
    line = shape((wide_y, LANES), f32)
    tail, edge, down, up = call(
        edge_tail_kernel,
        (shape((wide_x, 8, LANES), f32), shape((groups, wide_y, LANES), f32), line, line),
        (part, within, across),
    )
    lower = cycle(up, "gz", 1)
    upper = cycle(down, "gz", -1)
    for k in range(3, len(steps)):
        held = jnp.concatenate([held, received], axis=0)
        received = join(k, held)

    half = devices // 2
    depth = min(half, 16) * LANES
    rows_all = 16 * pl.cdiv(groups * wide_y, 16)
    field = pltpu.VMEM((planes, wide_y, LANES), f32)
    edges = (groups, wide_y, LANES)
    margin = pltpu.VMEM(edges, f32)
    kinds = pltpu.VMEM((5, wide_y, LANES), f32)
    block = shape((size_x, size_y, LANES), f32)
    direction, applied, stats = call(
        functools.partial(main_kernel, sizes, records, halves, slabs, size_x, size_y),
        (block, block, shape((devices, 1, LANES), f32)),
        (held, received, right_side, above, below, tail, edge, lower, upper),
        (
            pltpu.VMEM((3, devices, LANES), f32),
            pltpu.VMEM((half, LANES), f32),
            pltpu.VMEM((2, LANES, LANES), f32),
            pltpu.VMEM((rows_all, depth), bf16),
            pltpu.VMEM((depth, (SUBS + 1) * LANES), bf16),
            pltpu.VMEM((rows_all, (SUBS + 1) * LANES), f32),
            field, field, field, field, field, field, field, kinds, kinds, margin, margin, margin, margin,
        ),
        mib=28,
    )
    stats = lax.all_to_all(stats, AXES, 0, 0, tiled=True)
    return call(
        functools.partial(finish_kernel, sizes, records, halves, slabs),
        (block, block),
        (stats, held, received, direction, applied),
        results=shape,
    )


def solution(mesh):
    placed = (
        P("gx", "gy", "gz"),
        P(("gx", "gy", "gz"), None),
        P(("gx", "gy", "gz"), None),
        P(("gx", "gy", "gz"), None),
        P(("gx", "gy", "gz")),
    )
    sizes = tuple(mesh.shape[axis] for axis in AXES)

    def body(*operands):
        return shards(sizes, *operands)

    return jax.shard_map(
        body,
        mesh=mesh,
        in_specs=placed,
        out_specs=(P("gx", "gy", "gz"), P("gx", "gy", "gz")),
        check_vma=False,
    )
```
